128 devices in a mesh: epoch: 8 (over z_lo, x), strip: 16 (over z_hi, y, core).
Axes of the slice: x: 4, y: 4, z: 4 (z_hi: 2, z_lo: 2; z = z_hi * 2 + z_lo), core: 2. Of those that a mesh axis runs over, the one named last changes fastest.
Arguments:
- raw_tiles: float32 [8, 192, 256, 512], P('epoch', 'strip'), may hold values from -6 to 6
- tile_kind: int32 [8, 192], P('epoch', 'strip'), may hold values from 0 to 3
- tile_invvar: float32 [8, 192], P('epoch', 'strip'), may hold values from 0.2 to 5
- tile_heights: int32 [8, 8, 24], P('epoch'), may hold values from 1 to 256, 4096 in all within a row
- row_interp: float32 [4, 256, 256], replicated, may hold values from -0.4 to 1.9
- col_interp: float32 [4, 512, 512], replicated, may hold values from -0.4 to 1.9
- psf_profiles: float32 [2, 2, 31], replicated, may hold values from -1 to 1
- psf_poly: float32 [8, 2, 6], replicated, may hold values from -1 to 1
Outputs:
- difference: float32 [8, 4096, 4096], P('epoch', 'strip')
The draws below stay inside these ranges and needn't reach their ends.
Inputs may be any that keep to these rules, and one draw needn't show every extreme that they name: `tile_heights`: along the last dimension, the heights of one column block's tiles from the top of the patch down; they sum to 4096, and the tallest is exactly 256.
All inputs are finite; a program needn't handle non-finite values.
Results may differ from the reference program's by a relative error of at most 0.0003.
Values sent between devices are 32-bit elements; how exact they have to be, the bound alone decides.
A program may use at most 128 MiB of HBM per device.

```python
import math
import jax
import jax.numpy as jnp
import numpy as np
from jax import lax

NCOL = 4096
TH = 256
TW = 512
KINDS = 4
KSIZE = 31
CB = 8
TILES = 192
PER_COL = 24
NROW = 4096
EPOCHS = 8


def interp_band(key, kinds_count, order):
    first_key, second_key, third_key = jax.random.split(key, 3)
    offset = jnp.arange(order)[None, :] - jnp.arange(order)[:, None]
    distance = jnp.abs(offset)
    shape_table = jnp.array([0.0, 0.3, -0.1, 0.04], jnp.float32)
    profile = jnp.take(shape_table, jnp.minimum(distance, 3))
    nearby = (distance >= 1) & (distance <= 3)
    spread = 0.3 / jnp.sqrt(jnp.float32(order))
    factor = jax.random.uniform(first_key, (kinds_count, order, order), jnp.float32, 0.5, 1.5)
    diagonal = jax.random.uniform(second_key, (kinds_count, order), jnp.float32, 1.4, 1.6)
    dense = jax.random.normal(third_key, (kinds_count, order, order), jnp.float32) * spread
    dense = jnp.clip(dense, -0.19, 0.19)
    off_part = jnp.where(nearby[None], profile[None] * factor, 0.0) + jnp.where(distance[None] >= 1, dense, 0.0)
    return off_part + diagonal[:, :, None] * jnp.eye(order, dtype=jnp.float32)[None]


def draw_row_interp(key, part):
    return interp_band(jax.random.fold_in(key, 11), KINDS, TH)


def draw_col_interp(key, part):
    return interp_band(jax.random.fold_in(key, 23), KINDS, TW)


def touch_ends(values, key, least, top_value):
    place = [jax.random.randint(jax.random.fold_in(key, axis), (), 0, length) for axis, length in enumerate(values.shape)]
    widest = values.shape.index(max(values.shape))
    next_to = place[:widest] + [(place[widest] + 1) % values.shape[widest]] + place[widest + 1:]
    return values.at[tuple(place)].set(least).at[tuple(next_to)].set(top_value)


def levels(rng, shape, cuts, smallest, largest):
    level = 1.0
    for axis_at, parts in cuts:
        steps = jax.random.uniform(jax.random.fold_in(jax.random.fold_in(rng, 6), axis_at), (parts,), jnp.float32, smallest / len(cuts), largest / len(cuts))
        level = level * jnp.repeat(jnp.exp(steps), shape[axis_at] // parts).reshape((-1,) + (1,) * (len(shape) - 1 - axis_at))
    return level


def split_up(count, total, bound, slope):
    portions = [(1 << 20) // math.isqrt(standing ** slope) + 1 for standing in range(2, count + 1)]
    spare, counts = total - bound - (count - 1), [1] * (count - 1)
    while spare > 0:
        candidates = [i for i in range(count - 1) if counts[i] < bound]
        pool, budget = sum([portions[i] for i in candidates]), spare
        for i in candidates:
            more = min(bound - counts[i], max(1, budget * portions[i] // pool), spare)
            counts[i] = counts[i] + more
            spare = spare - more
    return np.array([bound] + counts)


def uneven_parts(stream_key, count, total, most, skew):
    if count == 2:
        one = jax.random.randint(stream_key, (), max(1, total - most), min(most, total - 1) + 1)
        return jnp.stack([one, total - one])
    tallies = jnp.asarray(split_up(count, total, most, skew), jnp.int32)
    twos = (count - 1) // 2
    giver, taker = tallies[1:1 + 2 * twos:2], tallies[2:2 + 2 * twos:2]
    room = jnp.minimum(giver - 1, most - taker)
    moved = jax.random.randint(jax.random.fold_in(stream_key, 1), (twos,), 0, 1 << 20) % (room + 1)
    tallies = tallies.at[1:1 + 2 * twos:2].set(giver - moved).at[2:2 + 2 * twos:2].set(taker + moved)
    return tallies[jax.random.permutation(jax.random.fold_in(stream_key, 2), count)]


def scatter_about(rng, dims, deviation, bound, cuts=(), held_as=jnp.bfloat16):
    loudness = levels(rng, dims, cuts, -0.22, 0.18) if cuts else 1.0
    values = jax.random.normal(rng, dims, jnp.float32) * deviation * loudness
    return jnp.minimum(jnp.maximum(values, -bound), bound).astype(held_as)


def setup_inputs(seed: int = 0) -> dict:
    key_of = jax.random.split(jax.random.key(seed), 9)
    return {
        "raw_tiles": scatter_about(key_of[0], (EPOCHS, TILES, TH, TW), 1.0, 6.0, ((0, 8), (1, 16)), jnp.float32),
        "tile_kind": touch_ends(jax.random.randint(key_of[1], (EPOCHS, TILES), 0, KINDS), jax.random.fold_in(key_of[1], 1), 0, KINDS - 1).astype(jnp.int32),
        "tile_invvar": jnp.clip(jnp.exp(math.log(5.0) - 3.218876 * jax.random.uniform(key_of[2], (EPOCHS, TILES), jnp.float32) ** levels(key_of[2], (EPOCHS, TILES), ((0, 8), (1, 16)), -0.2, 0.2)), 0.2, 5.0),
        "tile_heights": jax.vmap(lambda own: uneven_parts(own, PER_COL, NROW, TH, 2))(jax.random.split(key_of[3], EPOCHS * CB)).reshape((EPOCHS, CB, PER_COL)).astype(jnp.int32),
        "row_interp": draw_row_interp(jax.random.fold_in(key_of[8], 71), 0),
        "col_interp": draw_col_interp(jax.random.fold_in(key_of[8], 71), 0),
        "psf_profiles": scatter_about(key_of[6], (2, 2, KSIZE), KSIZE ** -0.5, 1.0, (), jnp.float32),
        "psf_poly": jnp.clip(jax.random.uniform(key_of[7], (EPOCHS, 2, 6), jnp.float32, -1.0, 1.0), -1.0, 1.0),
    }


precise = lax.Precision.HIGHEST


def positions(first_cell, length, extent):
    counter = (first_cell + jnp.arange(length)).astype(jnp.float32)
    return (2.0 * counter + 1.0) / extent - 1.0


def coeff_maps(poly_rows, row_coords, col_coords):
    row_term = row_coords[:, None]
    col_term = col_coords[None, :]
    terms = poly_rows[..., None, None]
    return (terms[..., 0, :, :] + terms[..., 1, :, :] * row_term + terms[..., 2, :, :] * col_term
            + terms[..., 3, :, :] * row_term * row_term + terms[..., 4, :, :] * row_term * col_term
            + terms[..., 5, :, :] * col_term * col_term)


def reference(raw_tiles, tile_kind, tile_invvar, tile_heights, row_interp, col_interp, psf_profiles, psf_poly):
    def sky_epoch(bundle):
        raw, tile_kinds, invvar, heights = bundle
        live_rows = jnp.arange(TH)[None, :] < heights.reshape(-1)[:, None]
        masked = jnp.where(live_rows[:, :, None], raw, 0.0)
        half_warped = jnp.einsum('tij,tjk->tik', row_interp[tile_kinds], masked, precision=precise)
        warped = jnp.einsum('tik,tlk->til', half_warped, col_interp[tile_kinds], precision=precise)
        starts = (jnp.cumsum(heights, axis=1) - heights).astype(jnp.int32)
        sky_rows = jnp.arange(NROW).astype(jnp.int32)
        covering = (jnp.sum((sky_rows[None, :, None] >= starts[:, None, :]).astype(jnp.int32), axis=2) - 1).astype(jnp.int32)
        picked_start = jnp.take_along_axis(starts, covering, axis=1)
        local_row = (sky_rows[None, :] - picked_start).astype(jnp.int32)
        tile_ids = (jnp.arange(CB)[:, None] * PER_COL + covering).astype(jnp.int32)
        flattened = warped.reshape(TILES * TH, TW)
        placed = jnp.take(flattened, (tile_ids * TH + local_row).reshape(-1), axis=0).reshape(CB, NROW, TW)
        science = jnp.transpose(placed, (1, 0, 2)).reshape(NROW, NCOL)
        weights = jnp.transpose(invvar[tile_ids])
        return science, weights

    sciences, weights = lax.map(sky_epoch, (raw_tiles, tile_kind, tile_invvar, tile_heights))
    weighted_sum = jnp.sum(sciences.reshape(EPOCHS, NROW, CB, TW) * weights[..., None], axis=0)
    weight_sum = jnp.sum(weights, axis=0)
    template = (weighted_sum / weight_sum[:, :, None]).reshape(NROW, NCOL)
    margin = KSIZE // 2
    padded = jnp.pad(template, margin)
    convolved = []
    for basis_index in range(2):
        along_rows = jnp.zeros((NROW, NCOL + 2 * margin), jnp.float32)
        for offset in range(KSIZE):
            along_rows = along_rows + psf_profiles[basis_index, 0, offset] * padded[offset:offset + NROW, :]
        result = jnp.zeros((NROW, NCOL), jnp.float32)
        for offset in range(KSIZE):
            result = result + psf_profiles[basis_index, 1, offset] * along_rows[:, offset:offset + NCOL]
        convolved.append(result)
    row_coords = positions(0, NROW, NROW)
    col_coords = positions(0, NCOL, NCOL)

    def subtract(bundle):
        science, poly_rows = bundle
        coeffs = coeff_maps(poly_rows, row_coords, col_coords)
        return science - (coeffs[0] * convolved[0] + coeffs[1] * convolved[1])

    return lax.map(subtract, (sciences, psf_poly))
```

```python
import functools

import jax
import jax.numpy as jnp
from jax import lax
from jax.experimental import pallas as pl
from jax.experimental.pallas import tpu as pltpu
from jax.sharding import PartitionSpec as P

F32 = jnp.float32
BF16 = jnp.bfloat16
MESH = pl.DeviceIdType.MESH
TILES_DEV = 12
PER_COL = 24
LOCAL_ROWS = 3328
SPAN = 3072
MIB = 2**20


def split_hi_lo(value):
    hi = value.astype(BF16)
    lo = (value - hi.astype(F32)).astype(BF16)
    return hi, lo


def dot(a, b):
    return jnp.dot(a, b, preferred_element_type=F32)


def dot_t(a, b):
    return lax.dot_general(a, b, (((1,), (1,)), ((), ())), preferred_element_type=F32)


def warp_kernel(
    kinds, heights, invvar, x_ref, r_ref, c_ref, placed, wrows, r_hi, r_lo, c_hi, c_lo, tops
):
    t = pl.program_id(0)
    strip = lax.axis_index("strip")
    block, side = strip // 2, strip % 2

    @pl.when(t == 0)
    def _():
        for k in range(4):
            r_hi[k], r_lo[k] = split_hi_lo(r_ref[k])
            c_hi[k], c_lo[k] = split_hi_lo(c_ref[k])
        placed[...] = jnp.zeros_like(placed)

        def above(i, top):
            @pl.when(i >= side * TILES_DEV)
            def _():
                tops[i - side * TILES_DEV] = top

            return top + heights[0, block, i]

        lax.fori_loop(0, (side + 1) * TILES_DEV, above, jnp.int32(0))
        row = lax.broadcasted_iota(jnp.int32, (32, 128), 0) * 128
        row = row + lax.broadcasted_iota(jnp.int32, (32, 128), 1)

        def weigh(i, acc):
            top = tops[i]
            live = (row >= top) & (row < top + heights[0, block, side * TILES_DEV + i])
            return jnp.where(live, invvar[0, i], acc)

        wrows[...] = lax.fori_loop(0, TILES_DEV, weigh, jnp.zeros((32, 128), F32))

    kind = kinds[0, t]
    height = heights[0, block, side * TILES_DEV + t]
    top = tops[t] - side * 1024
    live = lax.broadcasted_iota(jnp.int32, (256, 512), 0) < height
    x_hi, x_lo = split_hi_lo(jnp.where(live, x_ref[0, 0], 0.0))
    y = dot_t(x_hi, c_hi[kind]) + (dot_t(x_hi, c_lo[kind]) + dot_t(x_lo, c_hi[kind]))
    y_hi, y_lo = split_hi_lo(y)
    w = dot(r_hi[kind], y_hi) + (dot(r_hi[kind], y_lo) + dot(r_lo[kind], y_hi))
    w = jnp.where(live, w, 0.0)
    for p in range(4):
        placed[p, pl.ds(top, 256), :] = w[:, p * 128 : (p + 1) * 128]


def warp(raw_tiles, tile_kind, tile_invvar, tile_heights, row_interp, col_interp):
    smem = pl.BlockSpec(memory_space=pltpu.SMEM)
    whole = lambda shape: pl.BlockSpec(shape, lambda t: (0,) * len(shape))
    return pl.pallas_call(
        warp_kernel,
        grid=(TILES_DEV,),
        out_shape=(
            jax.ShapeDtypeStruct((4, LOCAL_ROWS, 128), F32),
            jax.ShapeDtypeStruct((32, 128), F32),
        ),
        in_specs=[
            smem,
            smem,
            smem,
            pl.BlockSpec((1, 1, 256, 512), lambda t: (0, t, 0, 0)),
            whole((4, 256, 256)),
            whole((4, 512, 512)),
        ],
        out_specs=(whole((4, LOCAL_ROWS, 128)), whole((32, 128))),
        scratch_shapes=[
            pltpu.VMEM((4, 256, 256), BF16),
            pltpu.VMEM((4, 256, 256), BF16),
            pltpu.VMEM((4, 512, 512), BF16),
            pltpu.VMEM((4, 512, 512), BF16),
            pltpu.SMEM((TILES_DEV,), jnp.int32),
        ],
        compiler_params=pltpu.CompilerParams(
            dimension_semantics=("arbitrary",), vmem_limit_bytes=48 * MIB
        ),
        name="warp",
    )(tile_kind, tile_heights, tile_invvar, raw_tiles, row_interp, col_interp)


def exchange_kernel(
    placed, wrows, sci, t_out, kept, prec, pb, wn, wbuf, sbuf, rbuf, zr, tt, tb,
    kept_sem, w_s, w_r, pair_s, pair_r, sci_s, sci_r, rs_s, rs_r, z_s, z_r,
    rel_s, rel_r, ag_s, ag_r, halo_s, halo_r, out_sem,
):
    e, s = lax.axis_index("epoch"), lax.axis_index("strip")
    zl, x = e // 4, e % 4
    c = s % 2
    pair = s + 1 - 2 * c
    q = 2 * x + zl
    x_right, x_left = zl * 4 + (x + 1) % 4, zl * 4 + (x + 3) % 4
    z_mate = (1 - zl) * 4 + x

    def send(src, dst, s_sem, r_sem, epoch, strip):
        copy = pltpu.make_async_remote_copy(
            src_ref=src, dst_ref=dst, send_sem=s_sem, recv_sem=r_sem,
            device_id={"epoch": epoch, "strip": strip}, device_id_type=MESH,
        )
        copy.start()

    def wait_on(ref, sem):
        pltpu.make_async_copy(ref, ref, sem).wait()

    def slab(ref, piece):
        return ref.at[:, pl.ds(piece * 256, 256), :]

    barrier = pltpu.get_barrier_semaphore()

    def greet(epoch, strip):
        pl.semaphore_signal(
            barrier, inc=1, device_id={"epoch": epoch, "strip": strip}, device_id_type=MESH
        )

    tb[:, 0:16, :] = jnp.zeros((32, 16, 128), F32)
    tb[:, 272:288, :] = jnp.zeros((32, 16, 128), F32)
    for k in range(1, 16):
        greet(e, (s + k) % 16)
    for k in range(1, 8):
        greet((e + k) % 8, s)
        greet((e + k) % 8, pair)
    for i in range(12):
        pltpu.make_async_copy(
            placed.at[pl.ds(2 * c, 2), pl.ds(i * 256, 256), :], slab(kept, i), kept_sem.at[i]
        ).start()
    pl.semaphore_wait(barrier, 29)

    for k in range(1, 16):
        epoch = (e + k % 8) % 8
        strip = s if k < 8 else pair
        send(wrows, wbuf.at[15 - k], w_s.at[k - 1], w_r.at[15 - k], epoch, strip)

    def piece_at(k):
        return (s // 2 + k // 2) % 8 * 2 + k % 2

    @pl.loop(0, 16)
    def _(k):
        i = piece_at(k) - 4 * c

        @pl.when((i >= 0) & (i < 12))
        def _():
            send(
                placed.at[pl.ds(2 * (1 - c), 2), pl.ds(i * 256, 256), :],
                slab(prec, i), pair_s.at[i], pair_r.at[i], e, pair,
            )

    for k in range(1, 16):
        wait_on(wbuf.at[15 - k], w_r.at[15 - k])
    mine = wrows[...] + wbuf[15 - 8]
    total = mine
    for k in range(1, 8):
        total = total + (wbuf[15 - k] + wbuf[15 - 8 - k])
    wbuf[15] = mine / total

    @pl.loop(0, 32)
    def _(i):
        row = jnp.broadcast_to(wbuf[15, pl.ds(i, 1), :], (128, 128))
        wn[pl.ds(i * 128, 128), :] = row.T

    def weighted(g, at):
        parts = []
        for j in range(2):
            rows = pl.ds((2 * g + j) * 256 + at * 64, 64)
            parts.append(pb[:, rows, :] * wn[rows, :][None])
        return parts

    def group_at(k):
        return (s // 2 + k) % 8

    def step_of(g):
        return 1 - 2 * (g % 2)

    @pl.loop(0, 8)
    def _(k):
        g = group_at(k)
        for j in range(2):
            r = 2 * g + j
            own, theirs = r - 4 * c, r - 4 * (1 - c)
            has_own = (own >= 0) & (own < 12)
            has_theirs = (theirs >= 0) & (theirs < 12)

            @pl.when(has_own)
            def _():
                wait_on(slab(kept, own), kept_sem.at[own])

            @pl.when(has_theirs)
            def _():
                wait_on(slab(prec, theirs), pair_r.at[theirs])

            @pl.when(has_own & has_theirs)
            def _():
                slab(pb, r)[...] = slab(kept, own)[...] + slab(prec, theirs)[...]

            @pl.when(has_own & jnp.logical_not(has_theirs))
            def _():
                slab(pb, r)[...] = slab(kept, own)[...]

            @pl.when(has_theirs & jnp.logical_not(has_own))
            def _():
                slab(pb, r)[...] = slab(prec, theirs)[...]

        step = step_of(g)
        parts = weighted(g, (x - step + 4) % 4)
        for j in range(2):
            sbuf[g, j] = parts[j]
        send(
            sbuf.at[g], rbuf.at[g, 0], rs_s.at[g], rs_r.at[g],
            zl * 4 + (x + step + 4) % 4, s,
        )
        for j in range(2):
            r = 2 * g + j

            @pl.when(r != s)
            def _():
                send(
                    slab(pb, r), sci.at[pl.ds(2 * s, 2)], sci_s.at[r], sci_r.at[s], e, r
                )

            @pl.when(r == s)
            def _():
                pltpu.make_async_copy(
                    slab(pb, r), sci.at[pl.ds(2 * s, 2)], sci_r.at[s]
                ).start()

    @pl.loop(0, 24)
    def _(m):
        k, g = m // 8, group_at(m % 8)
        step = step_of(g)
        wait_on(rbuf.at[g, k], rs_r.at[k * 8 + g])
        parts = weighted(g, (x - step * (2 + k) + 12) % 4)
        for j in range(2):
            rbuf[g, k, j] = rbuf[g, k, j] + parts[j]

        @pl.when(k < 2)
        def _():
            send(
                rbuf.at[g, k], rbuf.at[g, k + 1], rs_s.at[(k + 1) * 8 + g],
                rs_r.at[(k + 1) * 8 + g], zl * 4 + (x + step + 4) % 4, s,
            )

        @pl.when(k == 2)
        def _():
            send(
                rbuf.at[g, 2, :, :, pl.ds(32 * (1 - zl), 32), :], zr.at[g],
                z_s.at[g], z_r.at[g], z_mate, s,
            )

    @pl.loop(0, 8)
    def _(k):
        g = group_at(k)
        wait_on(zr.at[g], z_r.at[g])
        for j in range(2):
            r = 2 * g + j
            tt[r] = rbuf[g, 2, j, :, pl.ds(32 * zl, 32), :] + zr[g, j]
            there = tb.at[pl.ds(2 * s, 2), pl.ds(16 + 32 * q, 32), :]

            @pl.when(r != s)
            def _():
                send(tt.at[r], there, rel_s.at[r], rel_r.at[s], e, r)

            @pl.when(r == s)
            def _():
                pltpu.make_async_copy(tt.at[r], there, rel_r.at[s]).start()

    def seg(j, first, count):
        return tb.at[pl.ds(8 * j, 8), pl.ds(16 + first, count), :]

    own_rows, mate_rows = 32 * q, 32 * (2 * x + 1 - zl)

    @pl.loop(0, 4)
    def _(j):
        for i in range(4):
            source = 4 * j + i
            wait_on(
                tb.at[pl.ds(2 * source, 2), pl.ds(16 + 32 * q, 32), :], rel_r.at[source]
            )
        part = seg(j, own_rows, 32)
        send(part, part, ag_s.at[j], ag_r.at[j], z_mate, s)
        send(part, part, ag_s.at[4 + j], ag_r.at[4 + j], x_right, s)
        send(part, part, ag_s.at[8 + j], ag_r.at[8 + j], x_left, s)

    @pl.loop(0, 4)
    def _(j):
        part = seg(j, mate_rows, 32)
        wait_on(part, ag_r.at[j])
        send(part, part, ag_s.at[12 + j], ag_r.at[12 + j], x_right, s)
        send(part, part, ag_s.at[16 + j], ag_r.at[16 + j], x_left, s)

    @pl.loop(0, 4)
    def _(j):
        left, right = (x + 3) % 4, (x + 1) % 4
        wait_on(seg(j, 64 * left + 32 * zl, 32), ag_r.at[4 + j])
        wait_on(seg(j, 64 * left + 32 * (1 - zl), 32), ag_r.at[12 + j])
        wait_on(seg(j, 64 * right + 32 * zl, 32), ag_r.at[8 + j])
        wait_on(seg(j, 64 * right + 32 * (1 - zl), 32), ag_r.at[16 + j])

        @pl.when(j % 2 == 0)
        def _():
            part = seg(j, 64 * left, 64)
            send(part, part, ag_s.at[20 + j], ag_r.at[20 + j], x_right, s)

        @pl.when(j % 2 == 1)
        def _():
            part = seg(j, 64 * right, 64)
            send(part, part, ag_s.at[20 + j], ag_r.at[20 + j], x_left, s)

    @pl.loop(0, 4)
    def _(j):
        wait_on(seg(j, 64 * ((x + 2) % 4), 64), ag_r.at[20 + j])
        planes = pl.ds(8 * j, 8)

        @pl.when(s > 0)
        def _():
            send(
                tb.at[planes, 16:32, :], tb.at[planes, 272:288, :],
                halo_s.at[j], halo_r.at[j], e, s - 1,
            )

        @pl.when(s < 15)
        def _():
            send(
                tb.at[planes, 256:272, :], tb.at[planes, 0:16, :],
                halo_s.at[4 + j], halo_r.at[4 + j], e, s + 1,
            )

    @pl.loop(0, 4)
    def _(j):
        planes = pl.ds(8 * j, 8)

        @pl.when(s < 15)
        def _():
            wait_on(tb.at[planes, 272:288, :], halo_r.at[j])

        @pl.when(s > 0)
        def _():
            wait_on(tb.at[planes, 0:16, :], halo_r.at[4 + j])

        pltpu.make_async_copy(tb.at[planes], t_out.at[planes], out_sem.at[j]).start()

    for i in range(4):
        wait_on(tb.at[pl.ds(8 * i, 8)], out_sem.at[i])
    for k in range(15):
        wait_on(wrows, w_s.at[k])

    @pl.loop(0, 12)
    def _(i):
        wait_on(slab(prec, i), pair_s.at[i])

    @pl.loop(0, 16)
    def _(r):
        wait_on(sci.at[pl.ds(2 * r, 2)], sci_r.at[r])

        @pl.when(r != s)
        def _():
            wait_on(slab(pb, r), sci_s.at[r])
            wait_on(tt.at[r], rel_s.at[r])

    @pl.loop(0, 24)
    def _(m):
        wait_on(sbuf.at[0], rs_s.at[m])

    @pl.loop(0, 8)
    def _(g):
        wait_on(zr.at[g], z_s.at[g])

    @pl.loop(0, 20)
    def _(m):
        wait_on(seg(0, 0, 32), ag_s.at[m])

    @pl.loop(0, 4)
    def _(j):
        wait_on(seg(0, 0, 64), ag_s.at[20 + j])

        @pl.when(s > 0)
        def _():
            wait_on(tb.at[0:8, 0:16, :], halo_s.at[j])

        @pl.when(s < 15)
        def _():
            wait_on(tb.at[0:8, 0:16, :], halo_s.at[4 + j])


def exchange(placed, wrows):
    vmem = lambda *shape: pltpu.VMEM(shape, F32)
    dma = lambda count: pltpu.SemaphoreType.DMA((count,))
    return pl.pallas_call(
        exchange_kernel,
        out_shape=(
            jax.ShapeDtypeStruct((32, 256, 128), F32),
            jax.ShapeDtypeStruct((32, 288, 128), F32),
        ),
        in_specs=[
            pl.BlockSpec(memory_space=pl.ANY),
            pl.BlockSpec(memory_space=pltpu.VMEM),
        ],
        out_specs=(pl.BlockSpec(memory_space=pl.ANY), pl.BlockSpec(memory_space=pl.ANY)),
        scratch_shapes=[
            vmem(2, SPAN, 128),
            vmem(2, SPAN, 128),
            vmem(2, 4096, 128),
            vmem(4096, 128),
            vmem(16, 32, 128),
            vmem(8, 2, 2, 64, 128),
            vmem(8, 3, 2, 2, 64, 128),
            vmem(8, 2, 2, 32, 128),
            vmem(16, 2, 32, 128),
            vmem(32, 288, 128),
            dma(12),
            dma(15), dma(15),
            dma(12), dma(12),
            dma(16), dma(16),
            dma(24), dma(24),
            dma(8), dma(8),
            dma(16), dma(16),
            dma(24), dma(24),
            dma(8), dma(8),
            dma(4),
        ],
        compiler_params=pltpu.CompilerParams(
            collective_id=0, has_side_effects=True, vmem_limit_bytes=40 * MIB
        ),
        name="exchange",
    )(placed, wrows)


def match_kernel(prof, poly, main, before, after, sci, out, band, toep):
    j = pl.program_id(0)
    steps = pl.num_programs(0)
    e, s = lax.axis_index("epoch"), lax.axis_index("strip")

    def taps(offset, k, axis):
        def add(i, acc):
            return jnp.where(offset == i, prof[k, axis, i], acc)

        return lax.fori_loop(0, 31, add, jnp.zeros(offset.shape, F32), unroll=True)

    @pl.when(j == 0)
    def _():
        lane = lax.broadcasted_iota(jnp.int32, (128, 480), 1)
        section = (lane >= 160).astype(jnp.int32) + (lane >= 320).astype(jnp.int32)
        offset = lane - 160 * section - lax.broadcasted_iota(jnp.int32, (128, 480), 0) - 1
        for k in range(2):
            hi, lo = split_hi_lo(taps(offset, k, 0))
            band[128 * k : 128 * k + 128, :] = jnp.where(
                section == 1, lo.astype(F32), hi.astype(F32)
            ).astype(BF16)
        m = lax.broadcasted_iota(jnp.int32, (256, 128), 0)
        source = jnp.where(m < 192, m, m - 256)
        offset = source - lax.broadcasted_iota(jnp.int32, (256, 128), 1) + 15
        for k in range(2):
            hi, lo = split_hi_lo(taps(offset, k, 1))
            toep[k, :, 0:128] = hi
            toep[k, :, 128:256] = lo

    planes = [jnp.where(j > 0, before[0], 0.0)] + [main[p] for p in range(8)]
    planes.append(jnp.where(j < steps - 1, after[0], 0.0))
    rows = []
    t_hi, t_lo = split_hi_lo(jnp.concatenate(planes, axis=1))
    for half in range(2):
        at = slice(128 * half, 128 * half + 160)
        stacked = jnp.concatenate([t_hi[at], t_hi[at], t_lo[at]], axis=0)
        rows.append(dot(band[...], stacked))
    lane = lax.broadcasted_iota(jnp.int32, (256, 128), 1)
    conv = []
    for k in range(2):
        both = jnp.concatenate([part[128 * k : 128 * k + 128] for part in rows], axis=0)
        cut = [both[:, 128 * p : 128 * p + 128] for p in range(10)]
        inputs = [
            jnp.concatenate([cut[p], jnp.where(lane < 64, cut[p + 1], cut[p - 1])], axis=1)
            for p in range(1, 9)
        ]
        hi, lo = split_hi_lo(jnp.concatenate(inputs, axis=0))
        first = dot(hi, toep[k])
        conv.append(first[:, :128] + (first[:, 128:] + dot(lo, toep[k, :, 0:128])))
    row = lax.broadcasted_iota(jnp.int32, (256, 128), 0) + s * 256
    u = (2.0 * row.astype(F32) + 1.0) / 4096.0 - 1.0
    terms = [[poly[e, k, i] for i in range(6)] for k in range(2)]
    base = [t[0] + t[1] * u + t[3] * u * u for t in terms]
    slope = [t[2] + t[4] * u for t in terms]
    for p in range(8):
        col = lane + (j * 8 + p) * 128
        v = (2.0 * col.astype(F32) + 1.0) / 4096.0 - 1.0
        at = slice(256 * p, 256 * p + 256)
        coeff = [base[k] + v * (slope[k] + terms[k][5] * v) for k in range(2)]
        out[0, :, 128 * p : 128 * p + 128] = sci[p] - (
            coeff[0] * conv[0][at] + coeff[1] * conv[1][at]
        )


def match(profiles, poly, template, science):
    smem = pl.BlockSpec(memory_space=pltpu.SMEM)
    return pl.pallas_call(
        match_kernel,
        grid=(4,),
        out_shape=jax.ShapeDtypeStruct((1, 256, 4096), F32),
        in_specs=[
            smem,
            smem,
            pl.BlockSpec((8, 288, 128), lambda j: (j, 0, 0)),
            pl.BlockSpec((1, 288, 128), lambda j: (jnp.maximum(8 * j - 1, 0), 0, 0)),
            pl.BlockSpec((1, 288, 128), lambda j: (jnp.minimum(8 * j + 8, 31), 0, 0)),
            pl.BlockSpec((8, 256, 128), lambda j: (j, 0, 0)),
        ],
        out_specs=pl.BlockSpec((1, 256, 1024), lambda j: (0, 0, j)),
        scratch_shapes=[pltpu.VMEM((256, 480), BF16), pltpu.VMEM((2, 256, 256), BF16)],
        compiler_params=pltpu.CompilerParams(
            dimension_semantics=("arbitrary",), vmem_limit_bytes=48 * MIB
        ),
        name="match",
    )(profiles, poly, template, template, template, science)


def shards(
    raw_tiles, tile_kind, tile_invvar, tile_heights, row_interp, col_interp, psf_profiles, psf_poly
):
    placed, wrows = warp(
        raw_tiles, tile_kind, tile_invvar, tile_heights, row_interp, col_interp
    )
    science, template = exchange(placed, wrows)
    return match(psf_profiles, psf_poly, template, science)


def solution(mesh):
    in_specs = (
        P("epoch", "strip", None, None),
        P("epoch", "strip"),
        P("epoch", "strip"),
        P("epoch", None, None),
        P(),
        P(),
        P(),
        P(),
    )
    out_specs = P("epoch", "strip", None)
    return jax.shard_map(shards, mesh=mesh, in_specs=in_specs, out_specs=out_specs, check_vma=False)
```

```python
import functools

import jax
import jax.numpy as jnp
from jax import lax
from jax.experimental import pallas as pl
from jax.experimental.pallas import tpu as pltpu
from jax.sharding import PartitionSpec as P

F32 = jnp.float32
BF16 = jnp.bfloat16
MESH = pl.DeviceIdType.MESH
TILES_DEV = 12
PER_COL = 24
LOCAL_ROWS = 3328
SPAN = 3072
VMEM_BYTES = 67043328
ROW_SENDS = (
    ((0, 0, 1), (1, 0, 0), (0, 1, 0), (0, 3, 0)),
    ((1, 1, 0), (1, 3, 1)),
    ((0, 2, 0),),
    ((1, 2, 0), (0, 2, 1)),
    ((1, 1, 1), (1, 3, 0)),
    ((0, 1, 1), (0, 3, 1), (1, 0, 1), (1, 2, 1)),
)


def split_hi_lo(value):
    hi = value.astype(BF16)
    lo = (value - hi.astype(F32)).astype(BF16)
    return hi, lo


def dot(a, b):
    return jnp.dot(a, b, preferred_element_type=F32)


def dot_t(a, b):
    return lax.dot_general(a, b, (((1,), (1,)), ((), ())), preferred_element_type=F32)


def warp_kernel(
    kinds, heights, invvar, x_ref, r_ref, c_ref, placed, wrows, r_hi, r_lo, c_hi, c_lo, tops
):
    t = pl.program_id(0)
    strip = lax.axis_index("strip")
    block, side = strip // 2, strip % 2

    @pl.when(t == 0)
    def _():
        for k in range(4):
            r_hi[k], r_lo[k] = split_hi_lo(r_ref[k])
            c_hi[k], c_lo[k] = split_hi_lo(c_ref[k])
        placed[...] = jnp.zeros_like(placed)

        def above(i, top):
            @pl.when(i >= side * TILES_DEV)
            def _():
                tops[i - side * TILES_DEV] = top

            return top + heights[0, block, i]

        lax.fori_loop(0, (side + 1) * TILES_DEV, above, jnp.int32(0))
        row = lax.broadcasted_iota(jnp.int32, (32, 128), 0) * 128
        row = row + lax.broadcasted_iota(jnp.int32, (32, 128), 1)

        def weigh(i, acc):
            top = tops[i]
            live = (row >= top) & (row < top + heights[0, block, side * TILES_DEV + i])
            return jnp.where(live, invvar[0, i], acc)

        wrows[...] = lax.fori_loop(0, TILES_DEV, weigh, jnp.zeros((32, 128), F32))

    kind = kinds[0, t]
    height = heights[0, block, side * TILES_DEV + t]
    top = tops[t] - side * 1024
    live = lax.broadcasted_iota(jnp.int32, (256, 512), 0) < height
    x_hi, x_lo = split_hi_lo(jnp.where(live, x_ref[0, 0], 0.0))
    y = dot_t(x_hi, c_hi[kind]) + (dot_t(x_hi, c_lo[kind]) + dot_t(x_lo, c_hi[kind]))
    y_hi, y_lo = split_hi_lo(y)
    w = dot(r_hi[kind], y_hi) + (dot(r_hi[kind], y_lo) + dot(r_lo[kind], y_hi))
    w = jnp.where(live, w, 0.0)
    for p in range(4):
        placed[p, pl.ds(top, 256), :] = w[:, p * 128 : (p + 1) * 128]


def warp(raw_tiles, tile_kind, tile_invvar, tile_heights, row_interp, col_interp):
    smem = pl.BlockSpec(memory_space=pltpu.SMEM)
    whole = lambda shape: pl.BlockSpec(shape, lambda t: (0,) * len(shape))
    return pl.pallas_call(
        warp_kernel,
        grid=(TILES_DEV,),
        out_shape=(
            jax.ShapeDtypeStruct((4, LOCAL_ROWS, 128), F32),
            jax.ShapeDtypeStruct((32, 128), F32),
        ),
        in_specs=[
            smem,
            smem,
            smem,
            pl.BlockSpec((1, 1, 256, 512), lambda t: (0, t, 0, 0)),
            whole((4, 256, 256)),
            whole((4, 512, 512)),
        ],
        out_specs=(whole((4, LOCAL_ROWS, 128)), whole((32, 128))),
        scratch_shapes=[
            pltpu.VMEM((4, 256, 256), BF16),
            pltpu.VMEM((4, 256, 256), BF16),
            pltpu.VMEM((4, 512, 512), BF16),
            pltpu.VMEM((4, 512, 512), BF16),
            pltpu.SMEM((TILES_DEV,), jnp.int32),
        ],
        compiler_params=pltpu.CompilerParams(
            dimension_semantics=("arbitrary",), vmem_limit_bytes=VMEM_BYTES
        ),
        name="warp",
    )(tile_kind, tile_heights, tile_invvar, raw_tiles, row_interp, col_interp)


def exchange_kernel(
    placed, wrows, sci, t_out, kept, prec, pb, wn, wbuf, wi, sbuf, rbuf, zr, tt, tb,
    kept_sem, w_s, w_r, pair_s, pair_r, sci_s, sci_r, rs_s, rs_r, z_s, z_r,
    rel_s, rel_r, ag_s, ag_r, halo_s, halo_r, out_sem,
):
    e, s = lax.axis_index("epoch"), lax.axis_index("strip")
    zl, x = e // 4, e % 4
    c = s % 2
    pair = s + 1 - 2 * c
    q = 2 * x + zl
    x_right, x_left = zl * 4 + (x + 1) % 4, zl * 4 + (x + 3) % 4
    z_mate = (1 - zl) * 4 + x

    def send(src, dst, s_sem, r_sem, epoch, strip):
        copy = pltpu.make_async_remote_copy(
            src_ref=src, dst_ref=dst, send_sem=s_sem, recv_sem=r_sem,
            device_id={"epoch": epoch, "strip": strip}, device_id_type=MESH,
        )
        copy.start()

    def wait_on(ref, sem):
        pltpu.make_async_copy(ref, ref, sem).wait()

    def slab(ref, piece):
        return ref.at[:, pl.ds(piece * 256, 256), :]

    barrier = pltpu.get_barrier_semaphore()

    def greet(epoch, strip):
        pl.semaphore_signal(
            barrier, inc=1, device_id={"epoch": epoch, "strip": strip}, device_id_type=MESH
        )

    tb[:, 0:16, :] = jnp.zeros((32, 16, 128), F32)
    tb[:, 272:288, :] = jnp.zeros((32, 16, 128), F32)
    for k in range(1, 16):
        greet(e, (s + k) % 16)
    for k in range(1, 8):
        greet((e + k) % 8, s)
        greet((e + k) % 8, pair)
    for i in range(12):
        pltpu.make_async_copy(
            placed.at[pl.ds(2 * c, 2), pl.ds(i * 256, 256), :], slab(kept, i), kept_sem.at[i]
        ).start()
    pl.semaphore_wait(barrier, 29)

    for k in range(1, 16):
        epoch = (e + k % 8) % 8
        strip = s if k < 8 else pair
        send(wrows, wbuf.at[15 - k], w_s.at[k - 1], w_r.at[15 - k], epoch, strip)

    def piece_at(k):
        return (s // 2 + k // 2) % 8 * 2 + k % 2

    @pl.loop(0, 16)
    def _(k):
        i = piece_at(k) - 4 * c

        @pl.when((i >= 0) & (i < 12))
        def _():
            send(
                placed.at[pl.ds(2 * (1 - c), 2), pl.ds(i * 256, 256), :],
                slab(prec, i), pair_s.at[i], pair_r.at[i], e, pair,
            )

    wait_on(wbuf.at[7], w_r.at[7])
    wbuf[15] = wrows[...] + wbuf[7]

    @pl.loop(0, 32)
    def _(i):
        row = jnp.broadcast_to(wbuf[15, pl.ds(i, 1), :], (128, 128))
        wn[pl.ds(i * 128, 128), :] = row.T

    def group_at(k):
        return (s // 2 + k) % 8

    def step_of(g):
        return 1 - 2 * (g % 2)

    def weighted(h, g, j, at):
        rows = pl.ds((2 * g + j) * 256 + at * 64, 64)
        return pb[h, rows, :] * wn[rows, :]

    def pass_on(src, h, g, k):
        to = zl * 4 + (x + step_of(g) + 4) % 4
        at = 24 * h + 8 * k + g
        send(src, rbuf.at[h, g, k], rs_s.at[at], rs_r.at[at], to, s)

    def begin(h, g):
        for j in range(2):
            sbuf[h, g, j] = weighted(h, g, j, (x - step_of(g) + 4) % 4)
        pass_on(sbuf.at[h, g], h, g, 0)

    @pl.loop(0, 8)
    def _(k):
        g = group_at(k)
        for j in range(2):
            r = 2 * g + j
            own, theirs = r - 4 * c, r - 4 * (1 - c)
            has_own = (own >= 0) & (own < 12)
            has_theirs = (theirs >= 0) & (theirs < 12)

            @pl.when(has_own)
            def _():
                wait_on(slab(kept, own), kept_sem.at[own])

            @pl.when(has_theirs)
            def _():
                wait_on(slab(prec, theirs), pair_r.at[theirs])

            @pl.when(has_own & has_theirs)
            def _():
                slab(pb, r)[...] = slab(kept, own)[...] + slab(prec, theirs)[...]

            @pl.when(has_own & jnp.logical_not(has_theirs))
            def _():
                slab(pb, r)[...] = slab(kept, own)[...]

            @pl.when(has_theirs & jnp.logical_not(has_own))
            def _():
                slab(pb, r)[...] = slab(prec, theirs)[...]

        begin(0, g)

    def send_rows(batch):
        for dz, dy, dc in ROW_SENDS[batch]:
            r = (s // 8 + dz) % 2 * 8 + (s // 2 + dy) % 4 * 2 + (c + dc) % 2
            send(slab(pb, r), sci.at[pl.ds(2 * s, 2)], sci_s.at[r], sci_r.at[s], e, r)

    def ring_step(h, k):
        @pl.loop(0, 8)
        def _(i):
            g = group_at(i)
            wait_on(rbuf.at[h, g, k], rs_r.at[24 * h + 8 * k + g])
            at = (x - step_of(g) * (2 + k) + 12) % 4
            for j in range(2):
                rbuf[h, g, k, j] = rbuf[h, g, k, j] + weighted(h, g, j, at)
            if k < 2:
                pass_on(rbuf.at[h, g, k], h, g, k + 1)
            else:
                away = rbuf.at[h, g, 2, :, pl.ds(32 * (1 - zl), 32), :]
                send(away, zr.at[h, g], z_s.at[8 * h + g], z_r.at[8 * h + g], z_mate, s)

    def finish(h):
        there = tb.at[16 * h + s, pl.ds(16 + 32 * q, 32), :]

        @pl.loop(0, 8)
        def _(k):
            g = group_at(k)
            wait_on(zr.at[h, g], z_r.at[8 * h + g])
            for j in range(2):
                r = 2 * g + j
                inverse = wi[pl.ds(128 * r + 32 * (q % 4), 32), :]
                summed = rbuf[h, g, 2, j, pl.ds(32 * zl, 32), :] + zr[h, g, j]
                tt[h, r] = summed * inverse

                @pl.when(r != s)
                def _():
                    send(tt.at[h, r], there, rel_s.at[16 * h + r], rel_r.at[16 * h + s], e, r)

                @pl.when(r == s)
                def _():
                    pltpu.make_async_copy(tt.at[h, r], there, rel_r.at[16 * h + s]).start()

    def seg(j, first, count):
        return tb.at[pl.ds(8 * j, 8), pl.ds(16 + first, count), :]

    own_rows, mate_rows = 32 * q, 32 * (2 * x + 1 - zl)
    left, right = (x + 3) % 4, (x + 1) % 4

    def gather_own(h):
        for j in (2 * h, 2 * h + 1):
            @pl.loop(8 * j, 8 * j + 8)
            def _(i):
                wait_on(tb.at[i, pl.ds(16 + 32 * q, 32), :], rel_r.at[i])

            part = seg(j, own_rows, 32)
            send(part, part, ag_s.at[j], ag_r.at[j], z_mate, s)
            send(part, part, ag_s.at[4 + j], ag_r.at[4 + j], x_right, s)
            send(part, part, ag_s.at[8 + j], ag_r.at[8 + j], x_left, s)

    def gather_mate(h):
        for j in (2 * h, 2 * h + 1):
            part = seg(j, mate_rows, 32)
            wait_on(part, ag_r.at[j])
            send(part, part, ag_s.at[12 + j], ag_r.at[12 + j], x_right, s)
            send(part, part, ag_s.at[16 + j], ag_r.at[16 + j], x_left, s)

    def gather_far(h):
        for j in (2 * h, 2 * h + 1):
            wait_on(seg(j, 64 * left + 32 * zl, 32), ag_r.at[4 + j])
            wait_on(seg(j, 64 * left + 32 * (1 - zl), 32), ag_r.at[12 + j])
            wait_on(seg(j, 64 * right + 32 * zl, 32), ag_r.at[8 + j])
            wait_on(seg(j, 64 * right + 32 * (1 - zl), 32), ag_r.at[16 + j])
            if j % 2 == 0:
                part = seg(j, 64 * left, 64)
                send(part, part, ag_s.at[20 + j], ag_r.at[20 + j], x_right, s)
            else:
                part = seg(j, 64 * right, 64)
                send(part, part, ag_s.at[20 + j], ag_r.at[20 + j], x_left, s)

    def edges(h):
        for j in (2 * h, 2 * h + 1):
            wait_on(seg(j, 64 * ((x + 2) % 4), 64), ag_r.at[20 + j])
            planes = pl.ds(8 * j, 8)

            @pl.when(s > 0)
            def _():
                send(
                    tb.at[planes, 16:32, :], tb.at[planes, 272:288, :],
                    halo_s.at[j], halo_r.at[j], e, s - 1,
                )

            @pl.when(s < 15)
            def _():
                send(
                    tb.at[planes, 256:272, :], tb.at[planes, 0:16, :],
                    halo_s.at[4 + j], halo_r.at[4 + j], e, s + 1,
                )

    def leave(h):
        for j in (2 * h, 2 * h + 1):
            planes = pl.ds(8 * j, 8)

            @pl.when(s < 15)
            def _():
                wait_on(tb.at[planes, 272:288, :], halo_r.at[j])

            @pl.when(s > 0)
            def _():
                wait_on(tb.at[planes, 0:16, :], halo_r.at[4 + j])

            pltpu.make_async_copy(tb.at[planes], t_out.at[planes], out_sem.at[j]).start()

    send_rows(0)
    pltpu.make_async_copy(slab(pb, s), sci.at[pl.ds(2 * s, 2)], sci_r.at[s]).start()
    ring_step(0, 0)
    send_rows(1)
    ring_step(0, 1)

    @pl.loop(0, 8)
    def _(k):
        begin(1, group_at(k))

    send_rows(2)
    for k in range(1, 16):
        if k != 8:
            wait_on(wbuf.at[15 - k], w_r.at[15 - k])
    total = wbuf[15]
    for k in range(1, 8):
        total = total + (wbuf[15 - k] + wbuf[15 - 8 - k])
    wbuf[15] = 1.0 / total

    @pl.loop(0, 16)
    def _(r):
        row = jnp.broadcast_to(wbuf[15, pl.ds(2 * r + q // 4, 1), :], (128, 128))
        wi[pl.ds(128 * r, 128), :] = row.T

    ring_step(0, 2)
    send_rows(3)
    ring_step(1, 0)
    finish(0)
    send_rows(4)
    ring_step(1, 1)
    gather_own(0)
    ring_step(1, 2)
    gather_mate(0)
    finish(1)
    gather_far(0)
    gather_own(1)
    send_rows(5)
    gather_mate(1)
    edges(0)
    gather_far(1)
    leave(0)
    edges(1)
    leave(1)

    for i in range(4):
        wait_on(tb.at[pl.ds(8 * i, 8)], out_sem.at[i])
    for k in range(15):
        wait_on(wrows, w_s.at[k])

    @pl.loop(0, 12)
    def _(i):
        wait_on(slab(prec, i), pair_s.at[i])

    @pl.loop(0, 16)
    def _(r):
        wait_on(sci.at[pl.ds(2 * r, 2)], sci_r.at[r])

        @pl.when(r != s)
        def _():
            wait_on(slab(pb, r), sci_s.at[r])
            wait_on(tt.at[0, r], rel_s.at[r])
            wait_on(tt.at[1, r], rel_s.at[16 + r])

    @pl.loop(0, 48)
    def _(m):
        wait_on(sbuf.at[0, 0], rs_s.at[m])

    @pl.loop(0, 16)
    def _(g):
        wait_on(zr.at[0, 0], z_s.at[g])

    @pl.loop(0, 20)
    def _(m):
        wait_on(seg(0, 0, 32), ag_s.at[m])

    @pl.loop(0, 4)
    def _(j):
        wait_on(seg(0, 0, 64), ag_s.at[20 + j])

        @pl.when(s > 0)
        def _():
            wait_on(tb.at[0:8, 0:16, :], halo_s.at[j])

        @pl.when(s < 15)
        def _():
            wait_on(tb.at[0:8, 0:16, :], halo_s.at[4 + j])


def exchange(placed, wrows):
    vmem = lambda *shape: pltpu.VMEM(shape, F32)
    dma = lambda count: pltpu.SemaphoreType.DMA((count,))
    return pl.pallas_call(
        exchange_kernel,
        out_shape=(
            jax.ShapeDtypeStruct((32, 256, 128), F32),
            jax.ShapeDtypeStruct((32, 288, 128), F32),
        ),
        in_specs=[
            pl.BlockSpec(memory_space=pl.ANY),
            pl.BlockSpec(memory_space=pltpu.VMEM),
        ],
        out_specs=(pl.BlockSpec(memory_space=pl.ANY), pl.BlockSpec(memory_space=pl.ANY)),
        scratch_shapes=[
            vmem(2, SPAN, 128),
            vmem(2, SPAN, 128),
            vmem(2, 4096, 128),
            vmem(4096, 128),
            vmem(16, 32, 128),
            vmem(2048, 128),
            vmem(2, 8, 2, 64, 128),
            vmem(2, 8, 3, 2, 64, 128),
            vmem(2, 8, 2, 32, 128),
            vmem(2, 16, 32, 128),
            vmem(32, 288, 128),
            dma(12),
            dma(15), dma(15),
            dma(12), dma(12),
            dma(16), dma(16),
            dma(48), dma(48),
            dma(16), dma(16),
            dma(32), dma(32),
            dma(24), dma(24),
            dma(8), dma(8),
            dma(4),
        ],
        compiler_params=pltpu.CompilerParams(
            collective_id=0, has_side_effects=True, vmem_limit_bytes=VMEM_BYTES
        ),
        name="exchange",
    )(placed, wrows)


def match_kernel(prof, poly, even, odd, before, after, sci, out, band, toep):
    j = pl.program_id(0)
    steps = pl.num_programs(0)
    e, s = lax.axis_index("epoch"), lax.axis_index("strip")

    def taps(offset, k, axis):
        def add(i, acc):
            return jnp.where(offset == i, prof[k, axis, i], acc)

        return lax.fori_loop(0, 31, add, jnp.zeros(offset.shape, F32), unroll=True)

    @pl.when(j == 0)
    def _():
        lane = lax.broadcasted_iota(jnp.int32, (128, 480), 1)
        section = (lane >= 160).astype(jnp.int32) + (lane >= 320).astype(jnp.int32)
        offset = lane - 160 * section - lax.broadcasted_iota(jnp.int32, (128, 480), 0) - 1
        for k in range(2):
            hi, lo = split_hi_lo(taps(offset, k, 0))
            band[128 * k : 128 * k + 128, :] = jnp.where(
                section == 1, lo.astype(F32), hi.astype(F32)
            ).astype(BF16)
        m = lax.broadcasted_iota(jnp.int32, (256, 128), 0)
        source = jnp.where(m < 192, m, m - 256)
        offset = source - lax.broadcasted_iota(jnp.int32, (256, 128), 1) + 15
        for k in range(2):
            hi, lo = split_hi_lo(taps(offset, k, 1))
            toep[k, :, 0:128] = hi
            toep[k, :, 128:256] = lo

    planes = [jnp.where(j > 0, before[0], 0.0)] + [(even, odd)[p % 2][p // 2] for p in range(8)]
    planes.append(jnp.where(j < steps - 1, after[0], 0.0))
    rows = []
    t_hi, t_lo = split_hi_lo(jnp.concatenate(planes, axis=1))
    for half in range(2):
        at = slice(128 * half, 128 * half + 160)
        stacked = jnp.concatenate([t_hi[at], t_hi[at], t_lo[at]], axis=0)
        rows.append(dot(band[...], stacked))
    lane = lax.broadcasted_iota(jnp.int32, (256, 128), 1)
    conv = []
    for k in range(2):
        both = jnp.concatenate([part[128 * k : 128 * k + 128] for part in rows], axis=0)
        cut = [both[:, 128 * p : 128 * p + 128] for p in range(10)]
        inputs = [
            jnp.concatenate([cut[p], jnp.where(lane < 64, cut[p + 1], cut[p - 1])], axis=1)
            for p in range(1, 9)
        ]
        hi, lo = split_hi_lo(jnp.concatenate(inputs, axis=0))
        first = dot(hi, toep[k])
        conv.append(first[:, :128] + (first[:, 128:] + dot(lo, toep[k, :, 0:128])))
    row = lax.broadcasted_iota(jnp.int32, (256, 128), 0) + s * 256
    u = (2.0 * row.astype(F32) + 1.0) / 4096.0 - 1.0
    terms = [[poly[e, k, i] for i in range(6)] for k in range(2)]
    base = [t[0] + t[1] * u + t[3] * u * u for t in terms]
    slope = [t[2] + t[4] * u for t in terms]
    for p in range(8):
        col = lane + (j * 8 + p) * 128
        v = (2.0 * col.astype(F32) + 1.0) / 4096.0 - 1.0
        at = slice(256 * p, 256 * p + 256)
        coeff = [base[k] + v * (slope[k] + terms[k][5] * v) for k in range(2)]
        out[0, :, 128 * p : 128 * p + 128] = sci[p] - (
            coeff[0] * conv[0][at] + coeff[1] * conv[1][at]
        )


def match(profiles, poly, template, science):
    smem = pl.BlockSpec(memory_space=pltpu.SMEM)
    return pl.pallas_call(
        match_kernel,
        grid=(4,),
        out_shape=jax.ShapeDtypeStruct((1, 256, 4096), F32),
        in_specs=[
            smem,
            smem,
            pl.BlockSpec((4, 288, 128), lambda j: (j, 0, 0)),
            pl.BlockSpec((4, 288, 128), lambda j: (4 + j, 0, 0)),
            pl.BlockSpec((1, 288, 128), lambda j: (15 + 4 * j, 0, 0)),
            pl.BlockSpec((1, 288, 128), lambda j: (4 * j + 4, 0, 0)),
            pl.BlockSpec((8, 256, 128), lambda j: (j, 0, 0)),
        ],
        out_specs=pl.BlockSpec((1, 256, 1024), lambda j: (0, 0, j)),
        scratch_shapes=[pltpu.VMEM((256, 480), BF16), pltpu.VMEM((2, 256, 256), BF16)],
        compiler_params=pltpu.CompilerParams(
            dimension_semantics=("arbitrary",), vmem_limit_bytes=VMEM_BYTES
        ),
        name="match",
    )(profiles, poly, template, template, template, template, science)


def shards(
    raw_tiles, tile_kind, tile_invvar, tile_heights, row_interp, col_interp, psf_profiles, psf_poly
):
    placed, wrows = warp(
        raw_tiles, tile_kind, tile_invvar, tile_heights, row_interp, col_interp
    )
    science, template = exchange(placed, wrows)
    return match(psf_profiles, psf_poly, template, science)


def solution(mesh):
    in_specs = (
        P("epoch", "strip", None, None),
        P("epoch", "strip"),
        P("epoch", "strip"),
        P("epoch", None, None),
        P(),
        P(),
        P(),
        P(),
    )
    out_specs = P("epoch", "strip", None)
    return jax.shard_map(shards, mesh=mesh, in_specs=in_specs, out_specs=out_specs, check_vma=False)
```

```python
import functools

import jax
import jax.numpy as jnp
from jax import lax
from jax.experimental import pallas as pl
from jax.experimental.pallas import tpu as pltpu
from jax.sharding import PartitionSpec as P

F32 = jnp.float32
BF16 = jnp.bfloat16
MESH = pl.DeviceIdType.MESH
TILES_DEV = 12
PER_STEP = 2
LOCAL_ROWS = 3328
SPAN = 3072
VMEM_BYTES = 67043328
ROW_SENDS = (
    ((0, 0, 1), (1, 0, 0), (0, 1, 0), (0, 3, 0)),
    ((1, 1, 0), (1, 3, 1)),
    ((0, 2, 0),),
    ((1, 2, 0), (0, 2, 1)),
    ((1, 1, 1), (1, 3, 0)),
    ((0, 1, 1), (0, 3, 1), (1, 0, 1), (1, 2, 1)),
)


def split_hi_lo(value):
    hi = value.astype(BF16)
    lo = (value - hi.astype(F32)).astype(BF16)
    return hi, lo


def dot(a, b):
    return jnp.dot(a, b, preferred_element_type=F32)


def dot_t(a, b):
    return lax.dot_general(a, b, (((1,), (1,)), ((), ())), preferred_element_type=F32)


def warp_kernel(
    kinds, heights, invvar, x_ref, r_hbm, c_hbm, out, wrows,
    r_f32, c_f32, r_cat, c_cat, placed, tops, r_sem, c_sem, out_sem,
):
    t = pl.program_id(0)
    strip = lax.axis_index("strip")
    block, side = strip // 2, strip % 2

    def piece(i):
        rows = pl.ds(i * 256, 256)
        return pltpu.make_async_copy(placed.at[:, rows, :], out.at[:, rows, :], out_sem.at[i])

    @pl.when(t == 0)
    def _():
        loads = []
        for k in range(4):
            loads.append(pltpu.make_async_copy(c_hbm.at[k], c_f32.at[k], c_sem.at[k]))
            loads.append(pltpu.make_async_copy(r_hbm.at[k], r_f32.at[k], r_sem.at[k]))
        for load in loads:
            load.start()
        placed[...] = jnp.zeros_like(placed)

        def above(i, top):
            @pl.when(i >= side * TILES_DEV)
            def _():
                tops[i - side * TILES_DEV] = top

            return top + heights[0, block, i]

        tops[TILES_DEV] = lax.fori_loop(0, (side + 1) * TILES_DEV, above, jnp.int32(0))
        row = lax.broadcasted_iota(jnp.int32, (32, 128), 0) * 128
        row = row + lax.broadcasted_iota(jnp.int32, (32, 128), 1)

        def weigh(i, acc):
            live = (row >= tops[i]) & (row < tops[i + 1])
            return jnp.where(live, invvar[0, i], acc)

        wrows[...] = lax.fori_loop(0, TILES_DEV, weigh, jnp.zeros((32, 128), F32))
        for k in range(4):
            loads[2 * k].wait()
            hi, lo = split_hi_lo(c_f32[k].T)
            for i, part in enumerate((hi, lo, hi)):
                c_cat[k, 512 * i : 512 * i + 512, :] = part
            loads[2 * k + 1].wait()
            hi, lo = split_hi_lo(r_f32[k])
            for i, part in enumerate((hi, hi, lo)):
                r_cat[k, :, 256 * i : 256 * i + 256] = part

    places = []
    for i in range(PER_STEP):
        n = PER_STEP * t + i
        kind, top = kinds[0, n], tops[n] - side * 1024
        live = lax.broadcasted_iota(jnp.int32, (256, 512), 0) < tops[n + 1] - tops[n]
        hi, lo = split_hi_lo(jnp.where(live, x_ref[0, i], 0.0))
        y = dot(jnp.concatenate([hi, hi, lo], axis=1), c_cat[kind])
        places.append((kind, top, live, y))
    warped = []
    for kind, top, live, y in places:
        hi, lo = split_hi_lo(y)
        w = dot(r_cat[kind], jnp.concatenate([hi, lo, hi], axis=0))
        warped.append(jnp.where(live, w, 0.0))
    for (kind, top, live, y), w in zip(places, warped):
        for p in range(4):
            placed[p, pl.ds(top, 256), :] = w[:, p * 128 : (p + 1) * 128]

    last = t == pl.num_programs(0) - 1
    start, end = tops[PER_STEP * t], tops[PER_STEP * (t + 1)]
    first = jnp.where(t == 0, 0, (start - side * 1024) // 256)
    ready = jnp.where(last, 12, jnp.minimum((end - side * 1024) // 256, 12))

    @pl.loop(first, ready)
    def _(i):
        piece(i).start()

    @pl.when(last)
    def _():
        @pl.loop(0, 12)
        def _(i):
            piece(i).wait()


def warp(raw_tiles, tile_kind, tile_invvar, tile_heights, row_interp, col_interp):
    smem = pl.BlockSpec(memory_space=pltpu.SMEM)
    anywhere = pl.BlockSpec(memory_space=pl.ANY)
    return pl.pallas_call(
        warp_kernel,
        grid=(TILES_DEV // PER_STEP,),
        out_shape=(
            jax.ShapeDtypeStruct((4, SPAN, 128), F32),
            jax.ShapeDtypeStruct((32, 128), F32),
        ),
        in_specs=[
            smem,
            smem,
            smem,
            pl.BlockSpec((1, PER_STEP, 256, 512), lambda t: (0, t, 0, 0)),
            anywhere,
            anywhere,
        ],
        out_specs=(anywhere, pl.BlockSpec((32, 128), lambda t: (0, 0))),
        scratch_shapes=[
            pltpu.VMEM((4, 256, 256), F32),
            pltpu.VMEM((4, 512, 512), F32),
            pltpu.VMEM((4, 256, 768), BF16),
            pltpu.VMEM((4, 1536, 512), BF16),
            pltpu.VMEM((4, LOCAL_ROWS, 128), F32),
            pltpu.SMEM((TILES_DEV + 1,), jnp.int32),
            pltpu.SemaphoreType.DMA((4,)),
            pltpu.SemaphoreType.DMA((4,)),
            pltpu.SemaphoreType.DMA((12,)),
        ],
        compiler_params=pltpu.CompilerParams(
            dimension_semantics=("arbitrary",), vmem_limit_bytes=VMEM_BYTES
        ),
        name="warp",
    )(tile_kind, tile_heights, tile_invvar, raw_tiles, row_interp, col_interp)


def exchange_kernel(
    placed, wrows, prof, sci, t_out, band, toep, kept, prec, pb, wn, wbuf, wi, sbuf, rbuf, zr, tt, tb,
    kept_sem, w_s, w_r, pair_s, pair_r, sci_s, sci_r, rs_s, rs_r, z_s, z_r,
    rel_s, rel_r, ag_s, ag_r, halo_s, halo_r, out_sem,
):
    e, s = lax.axis_index("epoch"), lax.axis_index("strip")
    zl, x = e // 4, e % 4
    c = s % 2
    pair = s + 1 - 2 * c
    q = 2 * x + zl
    x_right, x_left = zl * 4 + (x + 1) % 4, zl * 4 + (x + 3) % 4
    z_mate = (1 - zl) * 4 + x

    def send(src, dst, s_sem, r_sem, epoch, strip):
        copy = pltpu.make_async_remote_copy(
            src_ref=src, dst_ref=dst, send_sem=s_sem, recv_sem=r_sem,
            device_id={"epoch": epoch, "strip": strip}, device_id_type=MESH,
        )
        copy.start()

    def wait_on(ref, sem):
        pltpu.make_async_copy(ref, ref, sem).wait()

    def slab(ref, piece):
        return ref.at[:, pl.ds(piece * 256, 256), :]

    barrier = pltpu.get_barrier_semaphore()

    def greet(epoch, strip):
        pl.semaphore_signal(
            barrier, inc=1, device_id={"epoch": epoch, "strip": strip}, device_id_type=MESH
        )

    tb[:, 0:16, :] = jnp.zeros((32, 16, 128), F32)
    tb[:, 272:288, :] = jnp.zeros((32, 16, 128), F32)
    for k in range(1, 16):
        greet(e, (s + k) % 16)
    for k in range(1, 8):
        greet((e + k) % 8, s)
        greet((e + k) % 8, pair)
    for i in range(12):
        pltpu.make_async_copy(
            placed.at[pl.ds(2 * c, 2), pl.ds(i * 256, 256), :], slab(kept, i), kept_sem.at[i]
        ).start()
    pl.semaphore_wait(barrier, 29)

    for k in range(1, 16):
        epoch = (e + k % 8) % 8
        strip = s if k < 8 else pair
        send(wrows, wbuf.at[15 - k], w_s.at[k - 1], w_r.at[15 - k], epoch, strip)

    def piece_at(k):
        return (s // 2 + k // 2) % 8 * 2 + k % 2

    @pl.loop(0, 16)
    def _(k):
        i = piece_at(k) - 4 * c

        @pl.when((i >= 0) & (i < 12))
        def _():
            send(
                placed.at[pl.ds(2 * (1 - c), 2), pl.ds(i * 256, 256), :],
                slab(prec, i), pair_s.at[i], pair_r.at[i], e, pair,
            )

    wait_on(wbuf.at[7], w_r.at[7])
    wbuf[15] = wrows[...] + wbuf[7]

    @pl.loop(0, 32)
    def _(i):
        row = jnp.broadcast_to(wbuf[15, pl.ds(i, 1), :], (128, 128))
        wn[pl.ds(i * 128, 128), :] = row.T

    def group_at(k):
        return (s // 2 + k) % 8

    def step_of(g):
        return 1 - 2 * (g % 2)

    def weighted(h, g, j, at):
        rows = pl.ds((2 * g + j) * 256 + at * 64, 64)
        return pb[h, rows, :] * wn[rows, :]

    def pass_on(src, h, g, k):
        to = zl * 4 + (x + step_of(g) + 4) % 4
        at = 24 * h + 8 * k + g
        send(src, rbuf.at[h, g, k], rs_s.at[at], rs_r.at[at], to, s)

    def begin(h, g):
        for j in range(2):
            sbuf[h, g, j] = weighted(h, g, j, (x - step_of(g) + 4) % 4)
        pass_on(sbuf.at[h, g], h, g, 0)

    @pl.loop(0, 8)
    def _(k):
        g = group_at(k)
        for j in range(2):
            r = 2 * g + j
            own, theirs = r - 4 * c, r - 4 * (1 - c)
            has_own = (own >= 0) & (own < 12)
            has_theirs = (theirs >= 0) & (theirs < 12)

            @pl.when(has_own)
            def _():
                wait_on(slab(kept, own), kept_sem.at[own])

            @pl.when(has_theirs)
            def _():
                wait_on(slab(prec, theirs), pair_r.at[theirs])

            @pl.when(has_own & has_theirs)
            def _():
                slab(pb, r)[...] = slab(kept, own)[...] + slab(prec, theirs)[...]

            @pl.when(has_own & jnp.logical_not(has_theirs))
            def _():
                slab(pb, r)[...] = slab(kept, own)[...]

            @pl.when(has_theirs & jnp.logical_not(has_own))
            def _():
                slab(pb, r)[...] = slab(prec, theirs)[...]

        begin(0, g)

    def send_rows(batch):
        for dz, dy, dc in ROW_SENDS[batch]:
            r = (s // 8 + dz) % 2 * 8 + (s // 2 + dy) % 4 * 2 + (c + dc) % 2
            send(slab(pb, r), sci.at[pl.ds(2 * s, 2)], sci_s.at[r], sci_r.at[s], e, r)

    def ring_step(h, k):
        @pl.loop(0, 8)
        def _(i):
            g = group_at(i)
            wait_on(rbuf.at[h, g, k], rs_r.at[24 * h + 8 * k + g])
            at = (x - step_of(g) * (2 + k) + 12) % 4
            for j in range(2):
                rbuf[h, g, k, j] = rbuf[h, g, k, j] + weighted(h, g, j, at)
            if k < 2:
                pass_on(rbuf.at[h, g, k], h, g, k + 1)
            else:
                away = rbuf.at[h, g, 2, :, pl.ds(32 * (1 - zl), 32), :]
                send(away, zr.at[h, g], z_s.at[8 * h + g], z_r.at[8 * h + g], z_mate, s)

    def finish(h):
        there = tb.at[16 * h + s, pl.ds(16 + 32 * q, 32), :]

        @pl.loop(0, 8)
        def _(k):
            g = group_at(k)
            wait_on(zr.at[h, g], z_r.at[8 * h + g])
            for j in range(2):
                r = 2 * g + j
                inverse = wi[pl.ds(128 * r + 32 * (q % 4), 32), :]
                summed = rbuf[h, g, 2, j, pl.ds(32 * zl, 32), :] + zr[h, g, j]
                tt[h, r] = summed * inverse

                @pl.when(r != s)
                def _():
                    send(tt.at[h, r], there, rel_s.at[16 * h + r], rel_r.at[16 * h + s], e, r)

                @pl.when(r == s)
                def _():
                    pltpu.make_async_copy(tt.at[h, r], there, rel_r.at[16 * h + s]).start()

    def seg(j, first, count):
        return tb.at[pl.ds(8 * j, 8), pl.ds(16 + first, count), :]

    own_rows, mate_rows = 32 * q, 32 * (2 * x + 1 - zl)
    left, right = (x + 3) % 4, (x + 1) % 4

    def gather_own(h):
        for j in (2 * h, 2 * h + 1):
            @pl.loop(8 * j, 8 * j + 8)
            def _(i):
                wait_on(tb.at[i, pl.ds(16 + 32 * q, 32), :], rel_r.at[i])

            part = seg(j, own_rows, 32)
            send(part, part, ag_s.at[j], ag_r.at[j], z_mate, s)
            send(part, part, ag_s.at[4 + j], ag_r.at[4 + j], x_right, s)
            send(part, part, ag_s.at[8 + j], ag_r.at[8 + j], x_left, s)

    def gather_mate(h):
        for j in (2 * h, 2 * h + 1):
            part = seg(j, mate_rows, 32)
            wait_on(part, ag_r.at[j])
            send(part, part, ag_s.at[12 + j], ag_r.at[12 + j], x_right, s)
            send(part, part, ag_s.at[16 + j], ag_r.at[16 + j], x_left, s)

    def gather_far(h):
        for j in (2 * h, 2 * h + 1):
            wait_on(seg(j, 64 * left + 32 * zl, 32), ag_r.at[4 + j])
            wait_on(seg(j, 64 * left + 32 * (1 - zl), 32), ag_r.at[12 + j])
            wait_on(seg(j, 64 * right + 32 * zl, 32), ag_r.at[8 + j])
            wait_on(seg(j, 64 * right + 32 * (1 - zl), 32), ag_r.at[16 + j])
            if j % 2 == 0:
                part = seg(j, 64 * left, 64)
                send(part, part, ag_s.at[20 + j], ag_r.at[20 + j], x_right, s)
            else:
                part = seg(j, 64 * right, 64)
                send(part, part, ag_s.at[20 + j], ag_r.at[20 + j], x_left, s)

    def edges(h):
        for j in (2 * h, 2 * h + 1):
            wait_on(seg(j, 64 * ((x + 2) % 4), 64), ag_r.at[20 + j])
            planes = pl.ds(8 * j, 8)

            @pl.when(s > 0)
            def _():
                send(
                    tb.at[planes, 16:32, :], tb.at[planes, 272:288, :],
                    halo_s.at[j], halo_r.at[j], e, s - 1,
                )

            @pl.when(s < 15)
            def _():
                send(
                    tb.at[planes, 256:272, :], tb.at[planes, 0:16, :],
                    halo_s.at[4 + j], halo_r.at[4 + j], e, s + 1,
                )

    def leave(h):
        for j in (2 * h, 2 * h + 1):
            planes = pl.ds(8 * j, 8)

            @pl.when(s < 15)
            def _():
                wait_on(tb.at[planes, 272:288, :], halo_r.at[j])

            @pl.when(s > 0)
            def _():
                wait_on(tb.at[planes, 0:16, :], halo_r.at[4 + j])

            pltpu.make_async_copy(tb.at[planes], t_out.at[planes], out_sem.at[j]).start()

    def taps(offset, k, axis):
        acc = jnp.zeros(offset.shape, F32)
        for i in range(31):
            acc = jnp.where(offset == i, prof[k, axis, i], acc)
        return acc

    def build_bands():
        iota = lambda shape, axis: lax.broadcasted_iota(jnp.int32, shape, axis)
        lane = iota((128, 480), 1)
        section = jnp.where(lane >= 320, 2, jnp.where(lane >= 160, 1, 0))
        offset = lane - 160 * section - iota((128, 480), 0) - 1
        m = iota((256, 128), 0)
        offset_c = jnp.where(m < 192, m, m - 256) - iota((256, 128), 1) + 15
        for k in range(2):
            hi, lo = split_hi_lo(taps(offset, k, 0))
            both = jnp.where(section == 1, lo.astype(F32), hi.astype(F32))
            band[128 * k : 128 * k + 128, :] = both.astype(BF16)
            hi, lo = split_hi_lo(taps(offset_c, k, 1))
            toep[k, :, 0:128] = hi
            toep[k, :, 128:256] = lo

    send_rows(0)
    pltpu.make_async_copy(slab(pb, s), sci.at[pl.ds(2 * s, 2)], sci_r.at[s]).start()
    ring_step(0, 0)
    send_rows(1)
    ring_step(0, 1)

    @pl.loop(0, 8)
    def _(k):
        begin(1, group_at(k))

    send_rows(2)
    for k in range(1, 16):
        if k != 8:
            wait_on(wbuf.at[15 - k], w_r.at[15 - k])
    total = wbuf[15]
    for k in range(1, 8):
        total = total + (wbuf[15 - k] + wbuf[15 - 8 - k])
    wbuf[15] = 1.0 / total

    @pl.loop(0, 16)
    def _(r):
        row = jnp.broadcast_to(wbuf[15, pl.ds(2 * r + q // 4, 1), :], (128, 128))
        wi[pl.ds(128 * r, 128), :] = row.T

    build_bands()
    ring_step(0, 2)
    send_rows(3)
    ring_step(1, 0)
    finish(0)
    send_rows(4)
    ring_step(1, 1)
    gather_own(0)
    ring_step(1, 2)
    gather_mate(0)
    finish(1)
    gather_far(0)
    gather_own(1)
    send_rows(5)
    gather_mate(1)
    edges(0)
    gather_far(1)
    leave(0)
    edges(1)
    leave(1)

    for i in range(4):
        wait_on(tb.at[pl.ds(8 * i, 8)], out_sem.at[i])
    for k in range(15):
        wait_on(wrows, w_s.at[k])

    @pl.loop(0, 12)
    def _(i):
        wait_on(slab(prec, i), pair_s.at[i])

    @pl.loop(0, 16)
    def _(r):
        wait_on(sci.at[pl.ds(2 * r, 2)], sci_r.at[r])

        @pl.when(r != s)
        def _():
            wait_on(slab(pb, r), sci_s.at[r])
            wait_on(tt.at[0, r], rel_s.at[r])
            wait_on(tt.at[1, r], rel_s.at[16 + r])

    @pl.loop(0, 48)
    def _(m):
        wait_on(sbuf.at[0, 0], rs_s.at[m])

    @pl.loop(0, 16)
    def _(g):
        wait_on(zr.at[0, 0], z_s.at[g])

    @pl.loop(0, 20)
    def _(m):
        wait_on(seg(0, 0, 32), ag_s.at[m])

    @pl.loop(0, 4)
    def _(j):
        wait_on(seg(0, 0, 64), ag_s.at[20 + j])

        @pl.when(s > 0)
        def _():
            wait_on(tb.at[0:8, 0:16, :], halo_s.at[j])

        @pl.when(s < 15)
        def _():
            wait_on(tb.at[0:8, 0:16, :], halo_s.at[4 + j])


def exchange(placed, wrows, profiles):
    vmem = lambda *shape: pltpu.VMEM(shape, F32)
    dma = lambda count: pltpu.SemaphoreType.DMA((count,))
    return pl.pallas_call(
        exchange_kernel,
        out_shape=(
            jax.ShapeDtypeStruct((32, 256, 128), F32),
            jax.ShapeDtypeStruct((32, 288, 128), F32),
            jax.ShapeDtypeStruct((256, 480), BF16),
            jax.ShapeDtypeStruct((2, 256, 256), BF16),
        ),
        in_specs=[
            pl.BlockSpec(memory_space=pl.ANY),
            pl.BlockSpec(memory_space=pltpu.VMEM),
            pl.BlockSpec(memory_space=pltpu.SMEM),
        ],
        out_specs=(
            pl.BlockSpec(memory_space=pl.ANY),
            pl.BlockSpec(memory_space=pl.ANY),
            pl.BlockSpec(memory_space=pltpu.VMEM),
            pl.BlockSpec(memory_space=pltpu.VMEM),
        ),
        scratch_shapes=[
            vmem(2, SPAN, 128),
            vmem(2, SPAN, 128),
            vmem(2, 4096, 128),
            vmem(4096, 128),
            vmem(16, 32, 128),
            vmem(2048, 128),
            vmem(2, 8, 2, 64, 128),
            vmem(2, 8, 3, 2, 64, 128),
            vmem(2, 8, 2, 32, 128),
            vmem(2, 16, 32, 128),
            vmem(32, 288, 128),
            dma(12),
            dma(15), dma(15),
            dma(12), dma(12),
            dma(16), dma(16),
            dma(48), dma(48),
            dma(16), dma(16),
            dma(32), dma(32),
            dma(24), dma(24),
            dma(8), dma(8),
            dma(4),
        ],
        compiler_params=pltpu.CompilerParams(
            collective_id=0, has_side_effects=True, vmem_limit_bytes=VMEM_BYTES
        ),
        name="exchange",
    )(placed, wrows, profiles)


def match_kernel(band, toep, poly, even, odd, before, after, sci, out):
    j = pl.program_id(0)
    steps = pl.num_programs(0)
    e, s = lax.axis_index("epoch"), lax.axis_index("strip")

    planes = [jnp.where(j > 0, before[0], 0.0)] + [(even, odd)[p % 2][p // 2] for p in range(8)]
    planes.append(jnp.where(j < steps - 1, after[0], 0.0))
    rows = []
    t_hi, t_lo = split_hi_lo(jnp.concatenate(planes, axis=1))
    for half in range(2):
        at = slice(128 * half, 128 * half + 160)
        stacked = jnp.concatenate([t_hi[at], t_hi[at], t_lo[at]], axis=0)
        rows.append(dot(band[...], stacked))
    lane = lax.broadcasted_iota(jnp.int32, (256, 128), 1)
    conv = []
    for k in range(2):
        both = jnp.concatenate([part[128 * k : 128 * k + 128] for part in rows], axis=0)
        cut = [both[:, 128 * p : 128 * p + 128] for p in range(10)]
        inputs = [
            jnp.concatenate([cut[p], jnp.where(lane < 64, cut[p + 1], cut[p - 1])], axis=1)
            for p in range(1, 9)
        ]
        hi, lo = split_hi_lo(jnp.concatenate(inputs, axis=0))
        first = dot(hi, toep[k])
        conv.append(first[:, :128] + (first[:, 128:] + dot(lo, toep[k, :, 0:128])))
    row = lax.broadcasted_iota(jnp.int32, (256, 128), 0) + s * 256
    u = (2.0 * row.astype(F32) + 1.0) / 4096.0 - 1.0
    terms = [[poly[e, k, i] for i in range(6)] for k in range(2)]
    base = [t[0] + t[1] * u + t[3] * u * u for t in terms]
    slope = [t[2] + t[4] * u for t in terms]
    for p in range(8):
        col = lane + (j * 8 + p) * 128
        v = (2.0 * col.astype(F32) + 1.0) / 4096.0 - 1.0
        at = slice(256 * p, 256 * p + 256)
        coeff = [base[k] + v * (slope[k] + terms[k][5] * v) for k in range(2)]
        out[0, :, 128 * p : 128 * p + 128] = sci[p] - (
            coeff[0] * conv[0][at] + coeff[1] * conv[1][at]
        )


def match(band, toep, poly, template, science):
    smem = pl.BlockSpec(memory_space=pltpu.SMEM)
    return pl.pallas_call(
        match_kernel,
        grid=(4,),
        out_shape=jax.ShapeDtypeStruct((1, 256, 4096), F32),
        in_specs=[
            pl.BlockSpec((256, 480), lambda j: (0, 0)),
            pl.BlockSpec((2, 256, 256), lambda j: (0, 0, 0)),
            smem,
            pl.BlockSpec((4, 288, 128), lambda j: (j, 0, 0)),
            pl.BlockSpec((4, 288, 128), lambda j: (4 + j, 0, 0)),
            pl.BlockSpec((1, 288, 128), lambda j: (15 + 4 * j, 0, 0)),
            pl.BlockSpec((1, 288, 128), lambda j: (4 * j + 4, 0, 0)),
            pl.BlockSpec((8, 256, 128), lambda j: (j, 0, 0)),
        ],
        out_specs=pl.BlockSpec((1, 256, 1024), lambda j: (0, 0, j)),
        compiler_params=pltpu.CompilerParams(
            dimension_semantics=("arbitrary",), vmem_limit_bytes=VMEM_BYTES
        ),
        name="match",
    )(band, toep, poly, template, template, template, template, science)


def shards(
    raw_tiles, tile_kind, tile_invvar, tile_heights, row_interp, col_interp, psf_profiles, psf_poly
):
    placed, wrows = warp(
        raw_tiles, tile_kind, tile_invvar, tile_heights, row_interp, col_interp
    )
    science, template, band, toep = exchange(placed, wrows, psf_profiles)
    return match(band, toep, psf_poly, template, science)


def solution(mesh):
    in_specs = (
        P("epoch", "strip", None, None),
        P("epoch", "strip"),
        P("epoch", "strip"),
        P("epoch", None, None),
        P(),
        P(),
        P(),
        P(),
    )
    out_specs = P("epoch", "strip", None)
    return jax.shard_map(shards, mesh=mesh, in_specs=in_specs, out_specs=out_specs, check_vma=False)
```

```python
import functools

import jax
import jax.numpy as jnp
from jax import lax
from jax.experimental import pallas as pl
from jax.experimental.pallas import tpu as pltpu
from jax.sharding import PartitionSpec as P

F32 = jnp.float32
BF16 = jnp.bfloat16
MESH = pl.DeviceIdType.MESH
TILES_DEV = 12
PER_STEP = 2
LOCAL_ROWS = 3328
SPAN = 3072
VMEM_BYTES = 67043328
ROW_SENDS = (
    ((0, 0, 1), (1, 0, 0), (0, 1, 0), (0, 3, 0)),
    ((1, 1, 0), (1, 3, 1)),
    ((0, 2, 0),),
    ((1, 2, 0), (0, 2, 1)),
    ((1, 1, 1), (1, 3, 0)),
    ((0, 1, 1), (0, 3, 1), (1, 0, 1), (1, 2, 1)),
)


def split_hi_lo(value):
    hi = value.astype(BF16)
    lo = (value - hi.astype(F32)).astype(BF16)
    return hi, lo


def dot(a, b):
    return jnp.dot(a, b, preferred_element_type=F32)


def dot_t(a, b):
    return lax.dot_general(a, b, (((1,), (1,)), ((), ())), preferred_element_type=F32)


def warp_kernel(
    kinds, heights, invvar, x_ref, r_hbm, c_hbm, out, wrows,
    r_f32, c_f32, r_cat, c_cat, placed, tops, r_sem, c_sem, out_sem,
):
    t = pl.program_id(0)
    strip = lax.axis_index("strip")
    block, side = strip // 2, strip % 2

    def piece(i):
        rows = pl.ds(i * 256, 256)
        return pltpu.make_async_copy(placed.at[:, rows, :], out.at[:, rows, :], out_sem.at[i])

    @pl.when(t == 0)
    def _():
        loads = []
        for k in range(4):
            loads.append(pltpu.make_async_copy(c_hbm.at[k], c_f32.at[k], c_sem.at[k]))
            loads.append(pltpu.make_async_copy(r_hbm.at[k], r_f32.at[k], r_sem.at[k]))
        for load in loads:
            load.start()
        placed[...] = jnp.zeros_like(placed)

        def above(i, top):
            @pl.when(i >= side * TILES_DEV)
            def _():
                tops[i - side * TILES_DEV] = top

            return top + heights[0, block, i]

        tops[TILES_DEV] = lax.fori_loop(0, (side + 1) * TILES_DEV, above, jnp.int32(0))
        row = lax.broadcasted_iota(jnp.int32, (32, 128), 0) * 128
        row = row + lax.broadcasted_iota(jnp.int32, (32, 128), 1)

        def weigh(i, acc):
            live = (row >= tops[i]) & (row < tops[i + 1])
            return jnp.where(live, invvar[0, i], acc)

        wrows[...] = lax.fori_loop(0, TILES_DEV, weigh, jnp.zeros((32, 128), F32))
        for k in range(4):
            loads[2 * k].wait()
            hi, lo = split_hi_lo(c_f32[k].T)
            for i, part in enumerate((hi, lo, hi)):
                c_cat[k, 512 * i : 512 * i + 512, :] = part
            loads[2 * k + 1].wait()
            hi, lo = split_hi_lo(r_f32[k])
            for i, part in enumerate((hi, hi, lo)):
                r_cat[k, :, 256 * i : 256 * i + 256] = part

    places = []
    for i in range(PER_STEP):
        n = PER_STEP * t + i
        kind, top = kinds[0, n], tops[n] - side * 1024
        live = lax.broadcasted_iota(jnp.int32, (256, 512), 0) < tops[n + 1] - tops[n]
        hi, lo = split_hi_lo(jnp.where(live, x_ref[0, i], 0.0))
        y = dot(jnp.concatenate([hi, hi, lo], axis=1), c_cat[kind])
        places.append((kind, top, live, y))
    warped = []
    for kind, top, live, y in places:
        hi, lo = split_hi_lo(y)
        w = dot(r_cat[kind], jnp.concatenate([hi, lo, hi], axis=0))
        warped.append(jnp.where(live, w, 0.0))
    for (kind, top, live, y), w in zip(places, warped):
        for p in range(4):
            placed[p, pl.ds(top, 256), :] = w[:, p * 128 : (p + 1) * 128]

    last = t == pl.num_programs(0) - 1
    start, end = tops[PER_STEP * t], tops[PER_STEP * (t + 1)]
    first = jnp.where(t == 0, 0, (start - side * 1024) // 256)
    ready = jnp.where(last, 12, jnp.minimum((end - side * 1024) // 256, 12))

    @pl.loop(first, ready)
    def _(i):
        piece(i).start()

    @pl.when(last)
    def _():
        @pl.loop(0, 12)
        def _(i):
            piece(i).wait()


def warp(raw_tiles, tile_kind, tile_invvar, tile_heights, row_interp, col_interp):
    smem = pl.BlockSpec(memory_space=pltpu.SMEM)
    anywhere = pl.BlockSpec(memory_space=pl.ANY)
    return pl.pallas_call(
        warp_kernel,
        grid=(TILES_DEV // PER_STEP,),
        out_shape=(
            jax.ShapeDtypeStruct((4, SPAN, 128), F32),
            jax.ShapeDtypeStruct((32, 128), F32),
        ),
        in_specs=[
            smem,
            smem,
            smem,
            pl.BlockSpec((1, PER_STEP, 256, 512), lambda t: (0, t, 0, 0)),
            anywhere,
            anywhere,
        ],
        out_specs=(anywhere, pl.BlockSpec((32, 128), lambda t: (0, 0))),
        scratch_shapes=[
            pltpu.VMEM((4, 256, 256), F32),
            pltpu.VMEM((4, 512, 512), F32),
            pltpu.VMEM((4, 256, 768), BF16),
            pltpu.VMEM((4, 1536, 512), BF16),
            pltpu.VMEM((4, LOCAL_ROWS, 128), F32),
            pltpu.SMEM((TILES_DEV + 1,), jnp.int32),
            pltpu.SemaphoreType.DMA((4,)),
            pltpu.SemaphoreType.DMA((4,)),
            pltpu.SemaphoreType.DMA((12,)),
        ],
        compiler_params=pltpu.CompilerParams(
            dimension_semantics=("arbitrary",), vmem_limit_bytes=VMEM_BYTES
        ),
        name="warp",
    )(tile_kind, tile_heights, tile_invvar, raw_tiles, row_interp, col_interp)


def exchange_kernel(
    placed, wrows, prof, sci, t_out, band, toep, kept, prec, pb, wn, wbuf, wi, sbuf, rbuf, zr, tt, tb,
    kept_sem, w_s, w_r, pair_s, pair_r, sci_s, sci_r, rs_s, rs_r, z_s, z_r,
    rel_s, rel_r, ag_s, ag_r, halo_s, halo_r, out_sem,
):
    e, s = lax.axis_index("epoch"), lax.axis_index("strip")
    zl, x = e // 4, e % 4
    c = s % 2
    pair = s + 1 - 2 * c
    q = 2 * x + zl
    x_right, x_left = zl * 4 + (x + 1) % 4, zl * 4 + (x + 3) % 4
    z_mate = (1 - zl) * 4 + x

    def send(src, dst, s_sem, r_sem, epoch, strip):
        copy = pltpu.make_async_remote_copy(
            src_ref=src, dst_ref=dst, send_sem=s_sem, recv_sem=r_sem,
            device_id={"epoch": epoch, "strip": strip}, device_id_type=MESH,
        )
        copy.start()

    def wait_on(ref, sem):
        pltpu.make_async_copy(ref, ref, sem).wait()

    def slab(ref, piece):
        return ref.at[:, pl.ds(piece * 256, 256), :]

    barrier = pltpu.get_barrier_semaphore()

    def greet(epoch, strip):
        pl.semaphore_signal(
            barrier, inc=1, device_id={"epoch": epoch, "strip": strip}, device_id_type=MESH
        )

    tb[:, 0:16, :] = jnp.zeros((32, 16, 128), F32)
    tb[:, 272:288, :] = jnp.zeros((32, 16, 128), F32)
    for k in range(1, 16):
        greet(e, (s + k) % 16)
    for k in range(1, 8):
        greet((e + k) % 8, s)
        greet((e + k) % 8, pair)
    for i in range(12):
        pltpu.make_async_copy(
            placed.at[pl.ds(2 * c, 2), pl.ds(i * 256, 256), :], slab(kept, i), kept_sem.at[i]
        ).start()
    pl.semaphore_wait(barrier, 29)

    def send_weights(k):
        epoch = (e + k % 8) % 8
        strip = s if k < 8 else pair
        send(wrows, wbuf.at[15 - k], w_s.at[k - 1], w_r.at[15 - k], epoch, strip)

    send_weights(8)

    def piece_at(k):
        return (s // 2 + k // 2) % 8 * 2 + k % 2

    @pl.loop(0, 16)
    def _(k):
        i = piece_at(k) - 4 * c

        @pl.when((i >= 0) & (i < 12))
        def _():
            send(
                placed.at[pl.ds(2 * (1 - c), 2), pl.ds(i * 256, 256), :],
                slab(prec, i), pair_s.at[i], pair_r.at[i], e, pair,
            )

    for k in (1, 2, 3, 4, 5, 6, 7, 9, 10, 11, 12, 13, 14, 15):
        send_weights(k)

    wait_on(wbuf.at[7], w_r.at[7])
    wbuf[15] = wrows[...] + wbuf[7]

    @pl.loop(0, 32)
    def _(i):
        row = jnp.broadcast_to(wbuf[15, pl.ds(i, 1), :], (128, 128))
        wn[pl.ds(i * 128, 128), :] = row.T

    def group_at(k):
        return (s // 2 + k) % 8

    def step_of(g):
        return 1 - 2 * (g % 2)

    def weighted(h, g, j, at):
        rows = pl.ds((2 * g + j) * 256 + at * 64, 64)
        return pb[h, rows, :] * wn[rows, :]

    def pass_on(src, h, g, k):
        to = zl * 4 + (x + step_of(g) + 4) % 4
        at = 24 * h + 8 * k + g
        send(src, rbuf.at[h, g, k], rs_s.at[at], rs_r.at[at], to, s)

    def begin(h, g):
        for j in range(2):
            sbuf[h, g, j] = weighted(h, g, j, (x - step_of(g) + 4) % 4)
        pass_on(sbuf.at[h, g], h, g, 0)

    @pl.loop(0, 8)
    def _(k):
        g = group_at(k)
        for j in range(2):
            r = 2 * g + j
            own, theirs = r - 4 * c, r - 4 * (1 - c)
            has_own = (own >= 0) & (own < 12)
            has_theirs = (theirs >= 0) & (theirs < 12)

            @pl.when(has_own)
            def _():
                wait_on(slab(kept, own), kept_sem.at[own])

            @pl.when(has_theirs)
            def _():
                wait_on(slab(prec, theirs), pair_r.at[theirs])

            @pl.when(has_own & has_theirs)
            def _():
                slab(pb, r)[...] = slab(kept, own)[...] + slab(prec, theirs)[...]

            @pl.when(has_own & jnp.logical_not(has_theirs))
            def _():
                slab(pb, r)[...] = slab(kept, own)[...]

            @pl.when(has_theirs & jnp.logical_not(has_own))
            def _():
                slab(pb, r)[...] = slab(prec, theirs)[...]

        begin(0, g)

    def send_rows(batch):
        for dz, dy, dc in ROW_SENDS[batch]:
            r = (s // 8 + dz) % 2 * 8 + (s // 2 + dy) % 4 * 2 + (c + dc) % 2
            send(slab(pb, r), sci.at[pl.ds(2 * s, 2)], sci_s.at[r], sci_r.at[s], e, r)

    def ring_step(h, k):
        @pl.loop(0, 8)
        def _(i):
            g = group_at(i)
            wait_on(rbuf.at[h, g, k], rs_r.at[24 * h + 8 * k + g])
            at = (x - step_of(g) * (2 + k) + 12) % 4
            for j in range(2):
                rbuf[h, g, k, j] = rbuf[h, g, k, j] + weighted(h, g, j, at)
            if k < 2:
                pass_on(rbuf.at[h, g, k], h, g, k + 1)
            else:
                away = rbuf.at[h, g, 2, :, pl.ds(32 * (1 - zl), 32), :]
                send(away, zr.at[h, g], z_s.at[8 * h + g], z_r.at[8 * h + g], z_mate, s)

    def finish(h):
        there = tb.at[16 * h + s, pl.ds(16 + 32 * q, 32), :]

        @pl.loop(0, 8)
        def _(k):
            g = group_at(k)
            wait_on(zr.at[h, g], z_r.at[8 * h + g])
            for j in range(2):
                r = 2 * g + j
                inverse = wi[pl.ds(128 * r + 32 * (q % 4), 32), :]
                summed = rbuf[h, g, 2, j, pl.ds(32 * zl, 32), :] + zr[h, g, j]
                tt[h, r] = summed * inverse

                @pl.when(r != s)
                def _():
                    send(tt.at[h, r], there, rel_s.at[16 * h + r], rel_r.at[16 * h + s], e, r)

                @pl.when(r == s)
                def _():
                    pltpu.make_async_copy(tt.at[h, r], there, rel_r.at[16 * h + s]).start()

    def seg(j, first, count):
        return tb.at[pl.ds(8 * j, 8), pl.ds(16 + first, count), :]

    own_rows, mate_rows = 32 * q, 32 * (2 * x + 1 - zl)
    left, right = (x + 3) % 4, (x + 1) % 4

    def gather_own(h):
        for j in (2 * h, 2 * h + 1):
            @pl.loop(8 * j, 8 * j + 8)
            def _(i):
                wait_on(tb.at[i, pl.ds(16 + 32 * q, 32), :], rel_r.at[i])

            part = seg(j, own_rows, 32)
            send(part, part, ag_s.at[j], ag_r.at[j], z_mate, s)
            send(part, part, ag_s.at[4 + j], ag_r.at[4 + j], x_right, s)
            send(part, part, ag_s.at[8 + j], ag_r.at[8 + j], x_left, s)

    def gather_mate(h):
        for j in (2 * h, 2 * h + 1):
            part = seg(j, mate_rows, 32)
            wait_on(part, ag_r.at[j])
            send(part, part, ag_s.at[12 + j], ag_r.at[12 + j], x_right, s)
            send(part, part, ag_s.at[16 + j], ag_r.at[16 + j], x_left, s)

    def gather_far(h):
        for j in (2 * h, 2 * h + 1):
            if j % 2 == 0:
                side, to, at = left, x_right, 4
            else:
                side, to, at = right, x_left, 8
            wait_on(seg(j, 64 * side + 32 * zl, 32), ag_r.at[at + j])
            wait_on(seg(j, 64 * side + 32 * (1 - zl), 32), ag_r.at[at + 8 + j])
            part = seg(j, 64 * side, 64)
            send(part, part, ag_s.at[20 + j], ag_r.at[20 + j], to, s)

    def edges(h):
        for j in (2 * h, 2 * h + 1):
            side, at = (right, 8) if j % 2 == 0 else (left, 4)
            wait_on(seg(j, 64 * side + 32 * zl, 32), ag_r.at[at + j])
            wait_on(seg(j, 64 * side + 32 * (1 - zl), 32), ag_r.at[at + 8 + j])
            wait_on(seg(j, 64 * ((x + 2) % 4), 64), ag_r.at[20 + j])
            planes = pl.ds(8 * j, 8)

            @pl.when(s > 0)
            def _():
                send(
                    tb.at[planes, 16:32, :], tb.at[planes, 272:288, :],
                    halo_s.at[j], halo_r.at[j], e, s - 1,
                )

            @pl.when(s < 15)
            def _():
                send(
                    tb.at[planes, 256:272, :], tb.at[planes, 0:16, :],
                    halo_s.at[4 + j], halo_r.at[4 + j], e, s + 1,
                )

    def leave(h):
        for j in (2 * h, 2 * h + 1):
            planes = pl.ds(8 * j, 8)

            @pl.when(s < 15)
            def _():
                wait_on(tb.at[planes, 272:288, :], halo_r.at[j])

            @pl.when(s > 0)
            def _():
                wait_on(tb.at[planes, 0:16, :], halo_r.at[4 + j])

            pltpu.make_async_copy(tb.at[planes], t_out.at[planes], out_sem.at[j]).start()

    def taps(offset, k, axis):
        acc = jnp.zeros(offset.shape, F32)
        for i in range(31):
            acc = jnp.where(offset == i, prof[k, axis, i], acc)
        return acc

    def build_bands():
        iota = lambda shape, axis: lax.broadcasted_iota(jnp.int32, shape, axis)
        lane = iota((128, 480), 1)
        section = jnp.where(lane >= 320, 2, jnp.where(lane >= 160, 1, 0))
        offset = lane - 160 * section - iota((128, 480), 0) - 1
        m = iota((256, 128), 0)
        offset_c = jnp.where(m < 192, m, m - 256) - iota((256, 128), 1) + 15
        for k in range(2):
            hi, lo = split_hi_lo(taps(offset, k, 0))
            both = jnp.where(section == 1, lo.astype(F32), hi.astype(F32))
            band[128 * k : 128 * k + 128, :] = both.astype(BF16)
            hi, lo = split_hi_lo(taps(offset_c, k, 1))
            toep[k, :, 0:128] = hi
            toep[k, :, 128:256] = lo

    send_rows(0)
    pltpu.make_async_copy(slab(pb, s), sci.at[pl.ds(2 * s, 2)], sci_r.at[s]).start()
    ring_step(0, 0)
    send_rows(1)
    ring_step(0, 1)

    @pl.loop(0, 8)
    def _(k):
        begin(1, group_at(k))

    send_rows(2)
    for k in range(1, 16):
        if k != 8:
            wait_on(wbuf.at[15 - k], w_r.at[15 - k])
    total = wbuf[15]
    for k in range(1, 8):
        total = total + (wbuf[15 - k] + wbuf[15 - 8 - k])
    wbuf[15] = 1.0 / total

    @pl.loop(0, 16)
    def _(r):
        row = jnp.broadcast_to(wbuf[15, pl.ds(2 * r + q // 4, 1), :], (128, 128))
        wi[pl.ds(128 * r, 128), :] = row.T

    build_bands()
    ring_step(0, 2)
    send_rows(3)
    ring_step(1, 0)
    finish(0)
    send_rows(4)
    ring_step(1, 1)
    gather_own(0)
    ring_step(1, 2)
    gather_mate(0)
    finish(1)
    gather_far(0)
    gather_own(1)
    send_rows(5)
    gather_mate(1)
    edges(0)
    gather_far(1)
    leave(0)
    edges(1)
    leave(1)

    for i in range(4):
        wait_on(tb.at[pl.ds(8 * i, 8)], out_sem.at[i])
    for k in range(15):
        wait_on(wrows, w_s.at[k])

    @pl.loop(0, 12)
    def _(i):
        wait_on(slab(prec, i), pair_s.at[i])

    @pl.loop(0, 16)
    def _(r):
        wait_on(sci.at[pl.ds(2 * r, 2)], sci_r.at[r])

        @pl.when(r != s)
        def _():
            wait_on(slab(pb, r), sci_s.at[r])
            wait_on(tt.at[0, r], rel_s.at[r])
            wait_on(tt.at[1, r], rel_s.at[16 + r])

    @pl.loop(0, 48)
    def _(m):
        wait_on(sbuf.at[0, 0], rs_s.at[m])

    @pl.loop(0, 16)
    def _(g):
        wait_on(zr.at[0, 0], z_s.at[g])

    @pl.loop(0, 20)
    def _(m):
        wait_on(seg(0, 0, 32), ag_s.at[m])

    @pl.loop(0, 4)
    def _(j):
        wait_on(seg(0, 0, 64), ag_s.at[20 + j])

        @pl.when(s > 0)
        def _():
            wait_on(tb.at[0:8, 0:16, :], halo_s.at[j])

        @pl.when(s < 15)
        def _():
            wait_on(tb.at[0:8, 0:16, :], halo_s.at[4 + j])


def exchange(placed, wrows, profiles):
    vmem = lambda *shape: pltpu.VMEM(shape, F32)
    dma = lambda count: pltpu.SemaphoreType.DMA((count,))
    return pl.pallas_call(
        exchange_kernel,
        out_shape=(
            jax.ShapeDtypeStruct((32, 256, 128), F32),
            jax.ShapeDtypeStruct((32, 288, 128), F32),
            jax.ShapeDtypeStruct((256, 480), BF16),
            jax.ShapeDtypeStruct((2, 256, 256), BF16),
        ),
        in_specs=[
            pl.BlockSpec(memory_space=pl.ANY),
            pl.BlockSpec(memory_space=pltpu.VMEM),
            pl.BlockSpec(memory_space=pltpu.SMEM),
        ],
        out_specs=(
            pl.BlockSpec(memory_space=pl.ANY),
            pl.BlockSpec(memory_space=pl.ANY),
            pl.BlockSpec(memory_space=pltpu.VMEM),
            pl.BlockSpec(memory_space=pltpu.VMEM),
        ),
        scratch_shapes=[
            vmem(2, SPAN, 128),
            vmem(2, SPAN, 128),
            vmem(2, 4096, 128),
            vmem(4096, 128),
            vmem(16, 32, 128),
            vmem(2048, 128),
            vmem(2, 8, 2, 64, 128),
            vmem(2, 8, 3, 2, 64, 128),
            vmem(2, 8, 2, 32, 128),
            vmem(2, 16, 32, 128),
            vmem(32, 288, 128),
            dma(12),
            dma(15), dma(15),
            dma(12), dma(12),
            dma(16), dma(16),
            dma(48), dma(48),
            dma(16), dma(16),
            dma(32), dma(32),
            dma(24), dma(24),
            dma(8), dma(8),
            dma(4),
        ],
        compiler_params=pltpu.CompilerParams(
            collective_id=0, has_side_effects=True, vmem_limit_bytes=VMEM_BYTES
        ),
        name="exchange",
    )(placed, wrows, profiles)


def match_kernel(band, toep, poly, even, odd, before, after, sci, out):
    j = pl.program_id(0)
    steps = pl.num_programs(0)
    e, s = lax.axis_index("epoch"), lax.axis_index("strip")

    planes = [jnp.where(j > 0, before[0], 0.0)] + [(even, odd)[p % 2][p // 2] for p in range(8)]
    planes.append(jnp.where(j < steps - 1, after[0], 0.0))
    rows = []
    t_hi, t_lo = split_hi_lo(jnp.concatenate(planes, axis=1))
    for half in range(2):
        at = slice(128 * half, 128 * half + 160)
        stacked = jnp.concatenate([t_hi[at], t_hi[at], t_lo[at]], axis=0)
        rows.append(dot(band[...], stacked))
    lane = lax.broadcasted_iota(jnp.int32, (256, 128), 1)
    conv = []
    for k in range(2):
        both = jnp.concatenate([part[128 * k : 128 * k + 128] for part in rows], axis=0)
        cut = [both[:, 128 * p : 128 * p + 128] for p in range(10)]
        inputs = [
            jnp.concatenate([cut[p], jnp.where(lane < 64, cut[p + 1], cut[p - 1])], axis=1)
            for p in range(1, 9)
        ]
        hi, lo = split_hi_lo(jnp.concatenate(inputs, axis=0))
        first = dot(hi, toep[k])
        conv.append(first[:, :128] + (first[:, 128:] + dot(lo, toep[k, :, 0:128])))
    row = lax.broadcasted_iota(jnp.int32, (256, 128), 0) + s * 256
    u = (2.0 * row.astype(F32) + 1.0) / 4096.0 - 1.0
    terms = [[poly[i, k, e] for i in range(6)] for k in range(2)]
    base = [t[0] + t[1] * u + t[3] * u * u for t in terms]
    slope = [t[2] + t[4] * u for t in terms]
    for p in range(8):
        col = lane + (j * 8 + p) * 128
        v = (2.0 * col.astype(F32) + 1.0) / 4096.0 - 1.0
        at = slice(256 * p, 256 * p + 256)
        coeff = [base[k] + v * (slope[k] + terms[k][5] * v) for k in range(2)]
        out[0, :, 128 * p : 128 * p + 128] = sci[p] - (
            coeff[0] * conv[0][at] + coeff[1] * conv[1][at]
        )


def match(band, toep, poly, template, science):
    smem = pl.BlockSpec(memory_space=pltpu.SMEM)
    return pl.pallas_call(
        match_kernel,
        grid=(4,),
        out_shape=jax.ShapeDtypeStruct((1, 256, 4096), F32),
        in_specs=[
            pl.BlockSpec((256, 480), lambda j: (0, 0)),
            pl.BlockSpec((2, 256, 256), lambda j: (0, 0, 0)),
            smem,
            pl.BlockSpec((4, 288, 128), lambda j: (j, 0, 0)),
            pl.BlockSpec((4, 288, 128), lambda j: (4 + j, 0, 0)),
            pl.BlockSpec((1, 288, 128), lambda j: (15 + 4 * j, 0, 0)),
            pl.BlockSpec((1, 288, 128), lambda j: (4 * j + 4, 0, 0)),
            pl.BlockSpec((8, 256, 128), lambda j: (j, 0, 0)),
        ],
        out_specs=pl.BlockSpec((1, 256, 1024), lambda j: (0, 0, j)),
        compiler_params=pltpu.CompilerParams(
            dimension_semantics=("arbitrary",), vmem_limit_bytes=VMEM_BYTES
        ),
        name="match",
    )(band, toep, poly, template, template, template, template, science)


def shards(
    raw_tiles, tile_kind, tile_invvar, tile_heights, row_interp, col_interp, psf_profiles, psf_poly
):
    placed, wrows = warp(
        raw_tiles, tile_kind, tile_invvar, tile_heights, row_interp, col_interp
    )
    science, template, band, toep = exchange(placed, wrows, psf_profiles)
    return match(band, toep, jnp.transpose(psf_poly, (2, 1, 0)), template, science)


def solution(mesh):
    in_specs = (
        P("epoch", "strip", None, None),
        P("epoch", "strip"),
        P("epoch", "strip"),
        P("epoch", None, None),
        P(),
        P(),
        P(),
        P(),
    )
    out_specs = P("epoch", "strip", None)
    return jax.shard_map(shards, mesh=mesh, in_specs=in_specs, out_specs=out_specs, check_vma=False)
```

```python
import functools

import jax
import jax.numpy as jnp
from jax import lax
from jax.experimental import pallas as pl
from jax.experimental.pallas import tpu as pltpu
from jax.sharding import PartitionSpec as P

F32 = jnp.float32
BF16 = jnp.bfloat16
MESH = pl.DeviceIdType.MESH
TILES_DEV = 12
PER_STEP = 3
LOCAL_ROWS = 3328
SPAN = 3072
VMEM_BYTES = 67043328
ROW_SENDS = (
    ((0, 0, 1), (1, 0, 0), (0, 1, 0), (0, 3, 0)),
    ((1, 1, 0), (1, 3, 1)),
    ((0, 2, 0),),
    ((1, 2, 0), (0, 2, 1)),
    ((1, 1, 1), (1, 3, 0)),
    ((0, 1, 1), (0, 3, 1), (1, 0, 1), (1, 2, 1)),
)


def split_hi_lo(value):
    hi = value.astype(BF16)
    lo = (value - hi.astype(F32)).astype(BF16)
    return hi, lo


def dot(a, b):
    return jnp.dot(a, b, preferred_element_type=F32)


def dot_t(a, b):
    return lax.dot_general(a, b, (((1,), (1,)), ((), ())), preferred_element_type=F32)


def warp_kernel(
    kinds, heights, invvar, x_ref, r_hbm, c_hbm, out, wrows,
    r_f32, c_f32, r_cat, c_cat, placed, tops, r_sem, c_sem, out_sem,
):
    t = pl.program_id(0)
    strip = lax.axis_index("strip")
    block, side = strip // 2, strip % 2

    def piece(i):
        rows = pl.ds(i * 256, 256)
        return pltpu.make_async_copy(placed.at[:, rows, :], out.at[:, rows, :], out_sem.at[i])

    @pl.when(t == 0)
    def _():
        loads = []
        for k in range(4):
            loads.append(pltpu.make_async_copy(c_hbm.at[k], c_f32.at[k], c_sem.at[k]))
            loads.append(pltpu.make_async_copy(r_hbm.at[k], r_f32.at[k], r_sem.at[k]))
        for load in loads:
            load.start()
        placed[...] = jnp.zeros_like(placed)

        def above(i, top):
            @pl.when(i >= side * TILES_DEV)
            def _():
                tops[i - side * TILES_DEV] = top

            return top + heights[0, block, i]

        tops[TILES_DEV] = lax.fori_loop(0, (side + 1) * TILES_DEV, above, jnp.int32(0))
        row = lax.broadcasted_iota(jnp.int32, (32, 128), 0) * 128
        row = row + lax.broadcasted_iota(jnp.int32, (32, 128), 1)

        def weigh(i, acc):
            live = (row >= tops[i]) & (row < tops[i + 1])
            return jnp.where(live, invvar[0, i], acc)

        wrows[...] = lax.fori_loop(0, TILES_DEV, weigh, jnp.zeros((32, 128), F32))
        for k in range(4):
            loads[2 * k].wait()
            hi, lo = split_hi_lo(c_f32[k].T)
            for i, part in enumerate((hi, lo, hi)):
                c_cat[k, 512 * i : 512 * i + 512, :] = part
            loads[2 * k + 1].wait()
            hi, lo = split_hi_lo(r_f32[k])
            for i, part in enumerate((hi, hi, lo)):
                r_cat[k, :, 256 * i : 256 * i + 256] = part

    places = []
    for i in range(PER_STEP):
        n = PER_STEP * t + i
        kind, top = kinds[0, n], tops[n] - side * 1024
        live = lax.broadcasted_iota(jnp.int32, (256, 512), 0) < tops[n + 1] - tops[n]
        hi, lo = split_hi_lo(jnp.where(live, x_ref[0, i], 0.0))
        y = dot(jnp.concatenate([hi, hi, lo], axis=1), c_cat[kind])
        places.append((kind, top, live, y))
    warped = []
    for kind, top, live, y in places:
        hi, lo = split_hi_lo(y)
        w = dot(r_cat[kind], jnp.concatenate([hi, lo, hi], axis=0))
        warped.append(jnp.where(live, w, 0.0))
    for (kind, top, live, y), w in zip(places, warped):
        for p in range(4):
            placed[p, pl.ds(top, 256), :] = w[:, p * 128 : (p + 1) * 128]

    last = t == pl.num_programs(0) - 1
    start, end = tops[PER_STEP * t], tops[PER_STEP * (t + 1)]
    first = jnp.where(t == 0, 0, (start - side * 1024) // 256)
    ready = jnp.where(last, 12, jnp.minimum((end - side * 1024) // 256, 12))

    @pl.loop(first, ready)
    def _(i):
        piece(i).start()

    @pl.when(last)
    def _():
        @pl.loop(0, 12)
        def _(i):
            piece(i).wait()


def warp(raw_tiles, tile_kind, tile_invvar, tile_heights, row_interp, col_interp):
    smem = pl.BlockSpec(memory_space=pltpu.SMEM)
    anywhere = pl.BlockSpec(memory_space=pl.ANY)
    return pl.pallas_call(
        warp_kernel,
        grid=(TILES_DEV // PER_STEP,),
        out_shape=(
            jax.ShapeDtypeStruct((4, SPAN, 128), F32),
            jax.ShapeDtypeStruct((32, 128), F32),
        ),
        in_specs=[
            smem,
            smem,
            smem,
            pl.BlockSpec((1, PER_STEP, 256, 512), lambda t: (0, t, 0, 0)),
            anywhere,
            anywhere,
        ],
        out_specs=(anywhere, pl.BlockSpec((32, 128), lambda t: (0, 0))),
        scratch_shapes=[
            pltpu.VMEM((4, 256, 256), F32),
            pltpu.VMEM((4, 512, 512), F32),
            pltpu.VMEM((4, 256, 768), BF16),
            pltpu.VMEM((4, 1536, 512), BF16),
            pltpu.VMEM((4, LOCAL_ROWS, 128), F32),
            pltpu.SMEM((TILES_DEV + 1,), jnp.int32),
            pltpu.SemaphoreType.DMA((4,)),
            pltpu.SemaphoreType.DMA((4,)),
            pltpu.SemaphoreType.DMA((12,)),
        ],
        compiler_params=pltpu.CompilerParams(
            dimension_semantics=("arbitrary",), vmem_limit_bytes=VMEM_BYTES
        ),
        name="warp",
    )(tile_kind, tile_heights, tile_invvar, raw_tiles, row_interp, col_interp)


def exchange_kernel(
    placed, wrows, prof, sci, t_out, band, toep, kept, prec, pb, wn, wbuf, wi, sbuf, rbuf, zr, tt, tb,
    kept_sem, w_s, w_r, pair_s, pair_r, sci_s, sci_r, rs_s, rs_r, z_s, z_r,
    rel_s, rel_r, ag_s, ag_r, halo_s, halo_r, out_sem,
):
    e, s = lax.axis_index("epoch"), lax.axis_index("strip")
    zl, x = e // 4, e % 4
    c = s % 2
    pair = s + 1 - 2 * c
    q = 2 * x + zl
    x_right, x_left = zl * 4 + (x + 1) % 4, zl * 4 + (x + 3) % 4
    z_mate = (1 - zl) * 4 + x

    def send(src, dst, s_sem, r_sem, epoch, strip):
        copy = pltpu.make_async_remote_copy(
            src_ref=src, dst_ref=dst, send_sem=s_sem, recv_sem=r_sem,
            device_id={"epoch": epoch, "strip": strip}, device_id_type=MESH,
        )
        copy.start()

    def wait_on(ref, sem):
        pltpu.make_async_copy(ref, ref, sem).wait()

    def slab(ref, piece):
        return ref.at[:, pl.ds(piece * 256, 256), :]

    barrier = pltpu.get_barrier_semaphore()

    def greet(epoch, strip):
        pl.semaphore_signal(
            barrier, inc=1, device_id={"epoch": epoch, "strip": strip}, device_id_type=MESH
        )

    tb[:, 0:16, :] = jnp.zeros((32, 16, 128), F32)
    tb[:, 272:288, :] = jnp.zeros((32, 16, 128), F32)
    for k in range(1, 16):
        greet(e, (s + k) % 16)
    for k in range(1, 8):
        greet((e + k) % 8, s)
        greet((e + k) % 8, pair)
    for i in range(12):
        pltpu.make_async_copy(
            placed.at[pl.ds(2 * c, 2), pl.ds(i * 256, 256), :], slab(kept, i), kept_sem.at[i]
        ).start()
    pl.semaphore_wait(barrier, 29)

    def send_weights(k):
        epoch = (e + k % 8) % 8
        strip = s if k < 8 else pair
        send(wrows, wbuf.at[15 - k], w_s.at[k - 1], w_r.at[15 - k], epoch, strip)

    send_weights(8)

    def piece_at(k):
        return (s // 2 + k // 2) % 8 * 2 + k % 2

    @pl.loop(0, 16)
    def _(k):
        i = piece_at(k) - 4 * c

        @pl.when((i >= 0) & (i < 12))
        def _():
            send(
                placed.at[pl.ds(2 * (1 - c), 2), pl.ds(i * 256, 256), :],
                slab(prec, i), pair_s.at[i], pair_r.at[i], e, pair,
            )

    for k in (1, 2, 3, 4, 5, 6, 7, 9, 10, 11, 12, 13, 14, 15):
        send_weights(k)

    wait_on(wbuf.at[7], w_r.at[7])
    wbuf[15] = wrows[...] + wbuf[7]

    @pl.loop(0, 32)
    def _(i):
        row = jnp.broadcast_to(wbuf[15, pl.ds(i, 1), :], (128, 128))
        wn[pl.ds(i * 128, 128), :] = row.T

    def group_at(k):
        return (s // 2 + k) % 8

    def step_of(g):
        return 1 - 2 * (g % 2)

    def weighted(h, g, j, at):
        rows = pl.ds((2 * g + j) * 256 + at * 64, 64)
        return pb[h, rows, :] * wn[rows, :]

    def pass_on(src, h, g, k):
        to = zl * 4 + (x + step_of(g) + 4) % 4
        at = 24 * h + 8 * k + g
        send(src, rbuf.at[h, g, k], rs_s.at[at], rs_r.at[at], to, s)

    def begin(h, g):
        for j in range(2):
            sbuf[h, g, j] = weighted(h, g, j, (x - step_of(g) + 4) % 4)
        pass_on(sbuf.at[h, g], h, g, 0)

    @pl.loop(0, 8)
    def _(k):
        g = group_at(k)
        for j in range(2):
            r = 2 * g + j
            own, theirs = r - 4 * c, r - 4 * (1 - c)
            has_own = (own >= 0) & (own < 12)
            has_theirs = (theirs >= 0) & (theirs < 12)

            @pl.when(has_own)
            def _():
                wait_on(slab(kept, own), kept_sem.at[own])

            @pl.when(has_theirs)
            def _():
                wait_on(slab(prec, theirs), pair_r.at[theirs])

            @pl.when(has_own & has_theirs)
            def _():
                slab(pb, r)[...] = slab(kept, own)[...] + slab(prec, theirs)[...]

            @pl.when(has_own & jnp.logical_not(has_theirs))
            def _():
                slab(pb, r)[...] = slab(kept, own)[...]

            @pl.when(has_theirs & jnp.logical_not(has_own))
            def _():
                slab(pb, r)[...] = slab(prec, theirs)[...]

        begin(0, g)

    def send_rows(batch):
        for dz, dy, dc in ROW_SENDS[batch]:
            r = (s // 8 + dz) % 2 * 8 + (s // 2 + dy) % 4 * 2 + (c + dc) % 2
            send(slab(pb, r), sci.at[pl.ds(2 * s, 2)], sci_s.at[r], sci_r.at[s], e, r)

    def ring_step(h, k):
        @pl.loop(0, 8)
        def _(i):
            g = group_at(i)
            wait_on(rbuf.at[h, g, k], rs_r.at[24 * h + 8 * k + g])
            at = (x - step_of(g) * (2 + k) + 12) % 4
            for j in range(2):
                rbuf[h, g, k, j] = rbuf[h, g, k, j] + weighted(h, g, j, at)
            if k < 2:
                pass_on(rbuf.at[h, g, k], h, g, k + 1)
            else:
                away = rbuf.at[h, g, 2, :, pl.ds(32 * (1 - zl), 32), :]
                send(away, zr.at[h, g], z_s.at[8 * h + g], z_r.at[8 * h + g], z_mate, s)

    def finish(h):
        there = tb.at[16 * h + s, pl.ds(16 + 32 * q, 32), :]

        @pl.loop(0, 8)
        def _(k):
            g = group_at(k)
            wait_on(zr.at[h, g], z_r.at[8 * h + g])
            for j in range(2):
                r = 2 * g + j
                inverse = wi[pl.ds(128 * r + 32 * (q % 4), 32), :]
                summed = rbuf[h, g, 2, j, pl.ds(32 * zl, 32), :] + zr[h, g, j]
                tt[h, r] = summed * inverse

                @pl.when(r != s)
                def _():
                    send(tt.at[h, r], there, rel_s.at[16 * h + r], rel_r.at[16 * h + s], e, r)

                @pl.when(r == s)
                def _():
                    pltpu.make_async_copy(tt.at[h, r], there, rel_r.at[16 * h + s]).start()

    def seg(j, first, count):
        return tb.at[pl.ds(8 * j, 8), pl.ds(16 + first, count), :]

    own_rows, mate_rows = 32 * q, 32 * (2 * x + 1 - zl)
    left, right = (x + 3) % 4, (x + 1) % 4

    def gather_own(h):
        for j in (2 * h, 2 * h + 1):
            @pl.loop(8 * j, 8 * j + 8)
            def _(i):
                wait_on(tb.at[i, pl.ds(16 + 32 * q, 32), :], rel_r.at[i])

            part = seg(j, own_rows, 32)
            send(part, part, ag_s.at[j], ag_r.at[j], z_mate, s)
            send(part, part, ag_s.at[4 + j], ag_r.at[4 + j], x_right, s)
            send(part, part, ag_s.at[8 + j], ag_r.at[8 + j], x_left, s)

    def gather_mate(h):
        for j in (2 * h, 2 * h + 1):
            part = seg(j, mate_rows, 32)
            wait_on(part, ag_r.at[j])
            send(part, part, ag_s.at[12 + j], ag_r.at[12 + j], x_right, s)
            send(part, part, ag_s.at[16 + j], ag_r.at[16 + j], x_left, s)

    def gather_far(h):
        for j in (2 * h, 2 * h + 1):
            if j % 2 == 0:
                side, to, at = left, x_right, 4
            else:
                side, to, at = right, x_left, 8
            wait_on(seg(j, 64 * side + 32 * zl, 32), ag_r.at[at + j])
            wait_on(seg(j, 64 * side + 32 * (1 - zl), 32), ag_r.at[at + 8 + j])
            part = seg(j, 64 * side, 64)
            send(part, part, ag_s.at[20 + j], ag_r.at[20 + j], to, s)

    def edges(h):
        for j in (2 * h, 2 * h + 1):
            side, at = (right, 8) if j % 2 == 0 else (left, 4)
            wait_on(seg(j, 64 * side + 32 * zl, 32), ag_r.at[at + j])
            wait_on(seg(j, 64 * side + 32 * (1 - zl), 32), ag_r.at[at + 8 + j])
            wait_on(seg(j, 64 * ((x + 2) % 4), 64), ag_r.at[20 + j])
            planes = pl.ds(8 * j, 8)

            @pl.when(s > 0)
            def _():
                send(
                    tb.at[planes, 16:32, :], tb.at[planes, 272:288, :],
                    halo_s.at[j], halo_r.at[j], e, s - 1,
                )

            @pl.when(s < 15)
            def _():
                send(
                    tb.at[planes, 256:272, :], tb.at[planes, 0:16, :],
                    halo_s.at[4 + j], halo_r.at[4 + j], e, s + 1,
                )

    def leave(h):
        for j in (2 * h, 2 * h + 1):
            planes = pl.ds(8 * j, 8)

            @pl.when(s < 15)
            def _():
                wait_on(tb.at[planes, 272:288, :], halo_r.at[j])

            @pl.when(s > 0)
            def _():
                wait_on(tb.at[planes, 0:16, :], halo_r.at[4 + j])

            pltpu.make_async_copy(tb.at[planes], t_out.at[planes], out_sem.at[j]).start()

    def taps(offset, k, axis):
        acc = jnp.zeros(offset.shape, F32)
        for i in range(31):
            acc = jnp.where(offset == i, prof[k, axis, i], acc)
        return acc

    def build_bands():
        iota = lambda shape, axis: lax.broadcasted_iota(jnp.int32, shape, axis)
        lane = iota((128, 480), 1)
        section = jnp.where(lane >= 320, 2, jnp.where(lane >= 160, 1, 0))
        offset = lane - 160 * section - iota((128, 480), 0) - 1
        m = iota((256, 128), 0)
        offset_c = jnp.where(m < 192, m, m - 256) - iota((256, 128), 1) + 15
        for k in range(2):
            hi, lo = split_hi_lo(taps(offset, k, 0))
            both = jnp.where(section == 1, lo.astype(F32), hi.astype(F32))
            band[128 * k : 128 * k + 128, :] = both.astype(BF16)
            hi, lo = split_hi_lo(taps(offset_c, k, 1))
            toep[k, :, 0:128] = hi
            toep[k, :, 128:256] = lo

    send_rows(0)
    pltpu.make_async_copy(slab(pb, s), sci.at[pl.ds(2 * s, 2)], sci_r.at[s]).start()
    ring_step(0, 0)
    send_rows(1)
    ring_step(0, 1)

    @pl.loop(0, 8)
    def _(k):
        begin(1, group_at(k))

    send_rows(2)
    for k in range(1, 16):
        if k != 8:
            wait_on(wbuf.at[15 - k], w_r.at[15 - k])
    total = wbuf[15]
    for k in range(1, 8):
        total = total + (wbuf[15 - k] + wbuf[15 - 8 - k])
    wbuf[15] = 1.0 / total

    @pl.loop(0, 16)
    def _(r):
        row = jnp.broadcast_to(wbuf[15, pl.ds(2 * r + q // 4, 1), :], (128, 128))
        wi[pl.ds(128 * r, 128), :] = row.T

    build_bands()
    ring_step(0, 2)
    send_rows(3)
    ring_step(1, 0)
    finish(0)
    send_rows(4)
    ring_step(1, 1)
    gather_own(0)
    ring_step(1, 2)
    gather_mate(0)
    finish(1)
    gather_far(0)
    gather_own(1)
    send_rows(5)
    gather_mate(1)
    edges(0)
    gather_far(1)
    leave(0)
    edges(1)
    leave(1)

    for i in range(4):
        wait_on(tb.at[pl.ds(8 * i, 8)], out_sem.at[i])
    for k in range(15):
        wait_on(wrows, w_s.at[k])

    @pl.loop(0, 12)
    def _(i):
        wait_on(slab(prec, i), pair_s.at[i])

    @pl.loop(0, 16)
    def _(r):
        wait_on(sci.at[pl.ds(2 * r, 2)], sci_r.at[r])

        @pl.when(r != s)
        def _():
            wait_on(slab(pb, r), sci_s.at[r])
            wait_on(tt.at[0, r], rel_s.at[r])
            wait_on(tt.at[1, r], rel_s.at[16 + r])

    @pl.loop(0, 48)
    def _(m):
        wait_on(sbuf.at[0, 0], rs_s.at[m])

    @pl.loop(0, 16)
    def _(g):
        wait_on(zr.at[0, 0], z_s.at[g])

    @pl.loop(0, 20)
    def _(m):
        wait_on(seg(0, 0, 32), ag_s.at[m])

    @pl.loop(0, 4)
    def _(j):
        wait_on(seg(0, 0, 64), ag_s.at[20 + j])

        @pl.when(s > 0)
        def _():
            wait_on(tb.at[0:8, 0:16, :], halo_s.at[j])

        @pl.when(s < 15)
        def _():
            wait_on(tb.at[0:8, 0:16, :], halo_s.at[4 + j])


def exchange(placed, wrows, profiles):
    vmem = lambda *shape: pltpu.VMEM(shape, F32)
    dma = lambda count: pltpu.SemaphoreType.DMA((count,))
    return pl.pallas_call(
        exchange_kernel,
        out_shape=(
            jax.ShapeDtypeStruct((32, 256, 128), F32),
            jax.ShapeDtypeStruct((32, 288, 128), F32),
            jax.ShapeDtypeStruct((256, 480), BF16),
            jax.ShapeDtypeStruct((2, 256, 256), BF16),
        ),
        in_specs=[
            pl.BlockSpec(memory_space=pl.ANY),
            pl.BlockSpec(memory_space=pltpu.VMEM),
            pl.BlockSpec(memory_space=pltpu.SMEM),
        ],
        out_specs=(
            pl.BlockSpec(memory_space=pl.ANY),
            pl.BlockSpec(memory_space=pl.ANY),
            pl.BlockSpec(memory_space=pltpu.VMEM),
            pl.BlockSpec(memory_space=pltpu.VMEM),
        ),
        scratch_shapes=[
            vmem(2, SPAN, 128),
            vmem(2, SPAN, 128),
            vmem(2, 4096, 128),
            vmem(4096, 128),
            vmem(16, 32, 128),
            vmem(2048, 128),
            vmem(2, 8, 2, 64, 128),
            vmem(2, 8, 3, 2, 64, 128),
            vmem(2, 8, 2, 32, 128),
            vmem(2, 16, 32, 128),
            vmem(32, 288, 128),
            dma(12),
            dma(15), dma(15),
            dma(12), dma(12),
            dma(16), dma(16),
            dma(48), dma(48),
            dma(16), dma(16),
            dma(32), dma(32),
            dma(24), dma(24),
            dma(8), dma(8),
            dma(4),
        ],
        compiler_params=pltpu.CompilerParams(
            collective_id=0, has_side_effects=True, vmem_limit_bytes=VMEM_BYTES
        ),
        name="exchange",
    )(placed, wrows, profiles)


def match_kernel(band, toep, poly, even, odd, before, after, sci, out):
    j = pl.program_id(0)
    steps = pl.num_programs(0)
    e, s = lax.axis_index("epoch"), lax.axis_index("strip")

    planes = [jnp.where(j > 0, before[0], 0.0)] + [(even, odd)[p % 2][p // 2] for p in range(8)]
    planes.append(jnp.where(j < steps - 1, after[0], 0.0))
    rows = []
    t_hi, t_lo = split_hi_lo(jnp.concatenate(planes, axis=1))
    for half in range(2):
        at = slice(128 * half, 128 * half + 160)
        stacked = jnp.concatenate([t_hi[at], t_hi[at], t_lo[at]], axis=0)
        rows.append(dot(band[...], stacked))
    lane = lax.broadcasted_iota(jnp.int32, (256, 128), 1)
    conv = []
    for k in range(2):
        both = jnp.concatenate([part[128 * k : 128 * k + 128] for part in rows], axis=0)
        cut = [both[:, 128 * p : 128 * p + 128] for p in range(10)]
        inputs = [
            jnp.concatenate([cut[p], jnp.where(lane < 64, cut[p + 1], cut[p - 1])], axis=1)
            for p in range(1, 9)
        ]
        hi, lo = split_hi_lo(jnp.concatenate(inputs, axis=0))
        first = dot(hi, toep[k])
        conv.append(first[:, :128] + (first[:, 128:] + dot(lo, toep[k, :, 0:128])))
    row = lax.broadcasted_iota(jnp.int32, (256, 128), 0) + s * 256
    u = (2.0 * row.astype(F32) + 1.0) / 4096.0 - 1.0
    terms = [[poly[i, k, e] for i in range(6)] for k in range(2)]
    base = [t[0] + t[1] * u + t[3] * u * u for t in terms]
    slope = [t[2] + t[4] * u for t in terms]
    for p in range(8):
        col = lane + (j * 8 + p) * 128
        v = (2.0 * col.astype(F32) + 1.0) / 4096.0 - 1.0
        at = slice(256 * p, 256 * p + 256)
        coeff = [base[k] + v * (slope[k] + terms[k][5] * v) for k in range(2)]
        out[0, :, 128 * p : 128 * p + 128] = sci[p] - (
            coeff[0] * conv[0][at] + coeff[1] * conv[1][at]
        )


def match(band, toep, poly, template, science):
    smem = pl.BlockSpec(memory_space=pltpu.SMEM)
    return pl.pallas_call(
        match_kernel,
        grid=(4,),
        out_shape=jax.ShapeDtypeStruct((1, 256, 4096), F32),
        in_specs=[
            pl.BlockSpec((256, 480), lambda j: (0, 0)),
            pl.BlockSpec((2, 256, 256), lambda j: (0, 0, 0)),
            smem,
            pl.BlockSpec((4, 288, 128), lambda j: (j, 0, 0)),
            pl.BlockSpec((4, 288, 128), lambda j: (4 + j, 0, 0)),
            pl.BlockSpec((1, 288, 128), lambda j: (15 + 4 * j, 0, 0)),
            pl.BlockSpec((1, 288, 128), lambda j: (4 * j + 4, 0, 0)),
            pl.BlockSpec((8, 256, 128), lambda j: (j, 0, 0)),
        ],
        out_specs=pl.BlockSpec((1, 256, 1024), lambda j: (0, 0, j)),
        compiler_params=pltpu.CompilerParams(
            dimension_semantics=("arbitrary",), vmem_limit_bytes=VMEM_BYTES
        ),
        name="match",
    )(band, toep, poly, template, template, template, template, science)


def shards(
    raw_tiles, tile_kind, tile_invvar, tile_heights, row_interp, col_interp, psf_profiles, psf_poly
):
    placed, wrows = warp(
        raw_tiles, tile_kind, tile_invvar, tile_heights, row_interp, col_interp
    )
    science, template, band, toep = exchange(placed, wrows, psf_profiles)
    return match(band, toep, jnp.transpose(psf_poly, (2, 1, 0)), template, science)


def solution(mesh):
    in_specs = (
        P("epoch", "strip", None, None),
        P("epoch", "strip"),
        P("epoch", "strip"),
        P("epoch", None, None),
        P(),
        P(),
        P(),
        P(),
    )
    out_specs = P("epoch", "strip", None)
    return jax.shard_map(shards, mesh=mesh, in_specs=in_specs, out_specs=out_specs, check_vma=False)
```
